128 devices in a mesh: grp: 4 (over z_lo, core), cell: 32 (over y, z_hi, x).
Axes of the slice: x: 4, y: 4, z: 4 (z_hi: 2, z_lo: 2; z = z_hi * 2 + z_lo), core: 2. Of those that a mesh axis runs over, the one named last changes fastest.
Arguments:
- theta: float32 [128, 256, 2048], P('grp', 'cell'), may hold values from 0.5 to 1.5
- density: float32 [128, 256, 2048], P('grp', 'cell'), may hold values from 0.05 to 0.8
- footprint: int32 [65536, 8], P('cell'), may hold values from 0 to 524287, as said below
- perturbed: float32 [128, 65536], P(None, 'cell'), may hold values from 0 to 6.4
- noise_var: float32 [65536], P('cell'), may hold values from 0.1 to 1
Outputs:
- theta_new: float32 [128, 256, 2048], P('grp', 'cell')
- predicted: float32 [128, 65536], P(None, 'cell')
The draws below stay inside these ranges and needn't reach their ends.
Inputs may be any that keep to these rules, and one draw needn't show every extreme that they name: `footprint`: each sensor's 8 cells form a patch of 2 neighbouring grid rows by 4 neighbouring columns, listed row by row; for the sensors numbered d * 2048 to (d + 1) * 2048 - 1 the patch's upper row is among grid rows d * 8 to (d + 1) * 8 - 1.
All inputs are finite; a program needn't handle non-finite values.
Results may differ from the reference program's by a relative error of at most 0.000082.
Values sent between devices are 32-bit elements; how exact they have to be, the bound alone decides.
No kernel may reach another device: no remote copies, remote signals or barrier semaphores. Data moves between devices by JAX's collectives and lax.ppermute only.
A program may use at most 128 MiB of HBM per device.

```python
import math
import jax
import jax.numpy as jnp
from jax import lax

CX = 8
NY = 2048
S_DEV = 2048
K = 8
STEPS = 2
J = 128
NX = 256
S = 65536


def draw_footprint(key, part):
    row_key = jax.random.fold_in(key, 11)
    col_key = jax.random.fold_in(key, 23)
    owner = jnp.arange(S, dtype=jnp.int32) // S_DEV
    offset = jax.random.randint(row_key, (S,), 0, CX, dtype=jnp.int32)
    upper = jnp.minimum(owner * CX + offset, NX - 2)
    width = K // 2
    left = jax.random.randint(col_key, (S,), 0, NY - width + 1, dtype=jnp.int32)
    sensor = jnp.arange(S, dtype=jnp.int32)
    upper = jnp.where(sensor == 0, 0, upper)
    left = jnp.where(sensor == 0, 0, left)
    upper = jnp.where(sensor == S - 1, NX - 2, upper)
    left = jnp.where(sensor == S - 1, NY - width, left)
    slot = jnp.arange(K, dtype=jnp.int32)
    rows = upper[:, None] + slot[None, :] // width
    cols = left[:, None] + slot[None, :] % width
    return (rows * NY + cols).astype(jnp.int32)


def block_levels(rng, shape, pieces, smallest, largest):
    def one(dim, blocks):
        draws = jax.random.uniform(jax.random.fold_in(jax.random.fold_in(rng, 6), dim), (blocks,), jnp.float32, smallest / len(pieces), largest / len(pieces))
        return jnp.repeat(jnp.exp(draws), shape[dim] // blocks).reshape((-1,) + (1,) * (len(shape) - dim - 1))

    factor_of = one(*pieces[0])
    for cut in pieces[1:]:
        factor_of = factor_of * one(*cut)
    return factor_of


def setup_inputs(seed: int = 0) -> dict:
    key_of = jax.random.split(jax.random.key(seed), 6)
    return {
        "theta": jnp.clip(0.5 + 1.0 * jax.random.uniform(key_of[0], (J, NX, NY), jnp.float32) ** block_levels(key_of[0], (J, NX, NY), ((0, 4), (1, 32)), -0.2, 0.2), 0.5, 1.5),
        "density": jnp.clip(0.05 + 0.75 * jax.random.uniform(key_of[1], (J, NX, NY), jnp.float32) ** block_levels(key_of[1], (J, NX, NY), ((0, 4), (1, 32)), -0.2, 0.2), 0.05, 0.8),
        "footprint": draw_footprint(jax.random.fold_in(key_of[5], 71), 0),
        "perturbed": jnp.clip(6.4 * jax.random.uniform(key_of[3], (J, S), jnp.float32) ** block_levels(key_of[3], (J, S), ((1, 32),), -0.2, 0.2), 0.0, 6.4),
        "noise_var": jnp.clip(jnp.exp(math.log(1.0) - 2.3025851 * jax.random.uniform(key_of[4], (S,), jnp.float32) ** block_levels(key_of[4], (S,), ((0, 32),), -0.2, 0.2)), 0.1, 1.0),
    }


def advance(rho, speed_pad):
    padded = jnp.pad(rho, ((0, 0), (1, 1), (1, 1)))
    flux_pad = speed_pad * padded * (1.0 - padded)
    center = flux_pad[:, 1:-1, 1:-1]
    flux = 2.0 * center - flux_pad[:, :-2, 1:-1] - flux_pad[:, 1:-1, :-2]
    spread = padded[:, 2:, 1:-1] + padded[:, :-2, 1:-1] + padded[:, 1:-1, 2:] + padded[:, 1:-1, :-2] - 4.0 * rho
    return rho - 0.2 * flux + 0.1 * spread

def reference(theta, density, footprint, perturbed, noise_var):
    speed_pad = jnp.pad(theta, ((0, 0), (1, 1), (1, 1)))
    rho = density
    for step in range(STEPS):
        rho = advance(rho, speed_pad)
    flat = rho.reshape(J, NX * NY)
    predicted = jnp.sum(jnp.take(flat, footprint, axis=1), axis=2)
    anomaly = predicted - jnp.mean(predicted, axis=0)
    weighted = anomaly / noise_var
    gram_p = jnp.dot(weighted.astype(jnp.float32), anomaly.T.astype(jnp.float32), precision=lax.Precision.HIGHEST, preferred_element_type=jnp.float32)
    gram_q = jnp.dot(weighted.astype(jnp.float32), (perturbed - predicted).T.astype(jnp.float32), precision=lax.Precision.HIGHEST, preferred_element_type=jnp.float32)
    system = (J - 1.0) * jnp.eye(J, dtype=jnp.float32) + gram_p
    factor = jnp.linalg.cholesky(system)
    mixing = jax.scipy.linalg.cho_solve((factor, True), gram_q)
    deviation = theta - jnp.mean(theta, axis=0)
    update = jnp.einsum('ij,ixy->jxy', mixing, deviation, precision=lax.Precision.HIGHEST)
    return (theta + update, predicted)
```

```python
import functools

import jax
import jax.numpy as jnp
from jax import lax
from jax.experimental import pallas as pl
from jax.experimental.pallas import tpu as pltpu
from jax.sharding import PartitionSpec as P

LANES = 128
F32 = jnp.float32


def along(axis, shift):
    count = lax.axis_size(axis)
    return [(i, i + shift) for i in range(count) if 0 <= i + shift < count]


def swapped(axis, bit):
    return [(i, i ^ bit) for i in range(lax.axis_size(axis))]


def vmem_params():
    return pltpu.CompilerParams(vmem_limit_bytes=56 * 1024 * 1024)


def outflow(speed, rho):
    return 0.2 * (speed * rho * (1.0 - rho)) + 0.1 * rho


def from_left(x):
    lane = lax.broadcasted_iota(jnp.int32, x.shape, 1)
    return jnp.where(lane == 0, 0.0, pltpu.roll(x, 1, 1))


def from_right(x):
    last = x.shape[1] - 1
    lane = lax.broadcasted_iota(jnp.int32, x.shape, 1)
    return jnp.where(lane == last, 0.0, pltpu.roll(x, last, 1))


def without_above(rho, out, below):
    return 0.8 * rho - 2.0 * out + from_left(out) + 0.1 * (below + from_right(rho))


def box4(x):
    n = x.shape[1]
    pair = x + pltpu.roll(x, n - 1, 1)
    return pair + pltpu.roll(pair, n - 2, 1)


def load_columns(source, target, sems):
    copies = []
    for b in range(source.shape[1] // LANES):
        copy = pltpu.make_async_copy(source.at[:, pl.ds(b * LANES, LANES)], target.at[b], sems.at[b])
        copy.start()
        copies.append(copy)
    return copies


def prep_kernel(members, rows, theta, rho, theta_t, rho_t, down, top, theta_in, rho_in, sems):
    waits = load_columns(rho, rho_in, sems.at[0]), load_columns(theta, theta_in, sems.at[1])
    for b in range(theta_in.shape[0]):
        at = slice(b * LANES, (b + 1) * LANES)
        waits[0][b].wait()
        waits[1][b].wait()
        for r in range(rows):
            speed = theta_in[b, pl.ds(r, members, stride=rows), :]
            now = rho_in[b, pl.ds(r, members, stride=rows), :]
            theta_t[r, :, at] = speed
            rho_t[r, :, at] = now
            if r == 0:
                top[:, at] = now
            if r == rows - 1:
                down[:, at] = outflow(speed, now)


def step1_kernel(theta, rho, above, below, rho1, down, top, part):
    rows, members, _ = rho.shape

    def chunk(c, carry):
        at = pl.ds(c * 8, 8)
        up = above[at, :]
        kept = None
        for r in range(rows):
            now = rho[r, at, :]
            under = rho[r + 1, at, :] if r + 1 < rows else below[at, :]
            speed = theta[r, at, :]
            out = outflow(speed, now)
            new = without_above(now, out, under) + up
            rho1[r, at, :] = new
            up = out
            if r == 0:
                top[at, :] = new
                kept = (new, outflow(speed, new))
            if r == 1:
                part[at, :] = without_above(kept[0], kept[1], new)
            if r == rows - 1:
                down[at, :] = outflow(speed, new)
        return carry

    lax.fori_loop(0, members // 8, chunk, 0)


def pick(table, first, count, pos_ref, start, out_ref):
    members = out_ref.shape[0]
    groups = pos_ref.shape[0]
    width = 4
    for g0 in range(0, groups, width):
        where = [jnp.broadcast_to(pos_ref[g : g + 1, :], (8, LANES)) for g in range(g0, g0 + width)]
        lane = [w & (LANES - 1) for w in where]
        block = [w >> 7 for w in where]
        init = tuple(
            start[m : m + 8, g * LANES : (g + 1) * LANES] if start is not None else jnp.zeros((8, LANES), F32)
            for g in range(g0, g0 + width)
            for m in range(0, members, 8)
        )

        def look(p, acc):
            rows = [table[p, m : m + 8, :] for m in range(0, members, 8)]
            new = []
            for k in range(width):
                hit = block[k] == p + first
                for i, row in enumerate(rows):
                    got = jnp.take_along_axis(row, lane[k], axis=1, mode="promise_in_bounds")
                    new.append(jnp.where(hit, got, acc[k * len(rows) + i]))
            return tuple(new)

        acc = lax.fori_loop(0, count, look, init, unroll=2)
        for k in range(width):
            for i in range(members // 8):
                g = g0 + k
                out_ref[i * 8 : i * 8 + 8, g * LANES : (g + 1) * LANES] = acc[k * (members // 8) + i]


def step2_kernel(theta, rho, above, below, pos, counts, rest, table):
    rows, members, columns = rho.shape
    blocks = columns // LANES

    def chunk(c, carry):
        at = pl.ds(c * 8, 8)
        up = above[at, :]
        last = None
        for r in range(rows):
            now = rho[r, at, :]
            under = rho[r + 1, at, :] if r + 1 < rows else below[at, :]
            out = outflow(theta[r, at, :], now)
            new = without_above(now, out, under) + up
            up = out
            if r > 0:
                sums = box4(last + new)
                for b in range(blocks):
                    table[(r - 1) * blocks + b, at, :] = sums[:, b * LANES : (b + 1) * LANES]
            if r == rows - 1:
                rest[at, :] = new + out
            last = new
        return carry

    lax.fori_loop(0, members // 8, chunk, 0)
    pick(table, 0, (rows - 1) * blocks, pos, None, counts)


def finish_kernel(first, rest, part, pos, counts, mine, table):
    members, columns = rest.shape
    blocks = columns // LANES
    for c in range(0, members, 8):
        sums = box4(rest[c : c + 8, :] + part[c : c + 8, :])
        for b in range(blocks):
            table[b, c : c + 8, :] = sums[:, b * LANES : (b + 1) * LANES]
    pick(table, first, blocks, pos, counts, mine)


def product_kernel(total, g_ref, own, core, chip, both, perturbed, noise, predicted, packed):
    members, sensors = own.shape
    g = g_ref[0]
    for step, piece in enumerate((own, core, chip, both)):
        predicted[pl.ds(pl.multiple_of((g ^ step) * members, members), members), :] = piece[...]
    width = 512
    acc = None
    for s in range(0, sensors, width):
        at = slice(s, s + width)
        all_counts = predicted[:, at]
        anomaly = all_counts - jnp.sum(all_counts, axis=0, keepdims=True) / total
        weighted = anomaly / noise[:, at]
        left = jnp.concatenate([anomaly, perturbed[:, at] - own[:, at]], axis=0)
        term = lax.dot_general(
            left, weighted, (((1,), (1,)), ((), ())), precision=lax.Precision.HIGHEST, preferred_element_type=F32
        )
        acc = term if acc is None else acc + term
    packed[...] = acc


def split(x):
    high = x.astype(jnp.bfloat16)
    return high, (x - high.astype(F32)).astype(jnp.bfloat16)


def update_kernel(rows, g_ref, mixing, own, core, chip, both, out, fields, new, sems, out_sems):
    members = own.shape[0] // rows
    g = g_ref[0]
    waits = [load_columns(piece, fields.at[k], sems.at[k]) for k, piece in enumerate((own, core, chip, both))]
    w = jnp.concatenate(
        [mixing[pl.ds(pl.multiple_of((g ^ step) * members, members), members), :] for step in range(4)], axis=0
    )
    wt = w.T
    wh, wl = split(wt)
    sent = []
    for b in range(new.shape[0]):
        for k in range(4):
            waits[k][b].wait()
        for r in range(rows):
            at = pl.ds(r, members, stride=rows)
            x = [fields[k, b, at, :] for k in range(4)]
            xh, xl = split(jnp.concatenate(x, axis=0))
            add = (
                jnp.dot(wh, xh, preferred_element_type=F32)
                + jnp.dot(wh, xl, preferred_element_type=F32)
                + jnp.dot(wl, xh, preferred_element_type=F32)
            )
            new[b, at, :] = x[0] + add
        copy = pltpu.make_async_copy(new.at[b], out.at[:, pl.ds(b * LANES, LANES)], out_sems.at[b])
        copy.start()
        sent.append(copy)
    for copy in sent:
        copy.wait()


def body(theta, density, footprint, perturbed, noise_var):
    members, rows, columns = theta.shape
    total = members * lax.axis_size("grp")
    sensors = footprint.shape[0]
    slab = rows * columns
    blocks = columns // LANES
    flat_theta = theta.reshape(members * rows, columns)
    flat_rho = density.reshape(members * rows, columns)
    g = lax.axis_index("grp").astype(jnp.int32).reshape(1)
    pos = (footprint[:, 0] - lax.axis_index("cell") * slab).reshape(sensors // LANES, LANES)

    row = jax.ShapeDtypeStruct((members, columns), F32)
    turned = jax.ShapeDtypeStruct((rows, members, columns), F32)
    anywhere = pl.BlockSpec(memory_space=pl.ANY)
    columns_of = pltpu.VMEM((blocks, members * rows, LANES), F32)
    theta_t, rho_t, down, top = pl.pallas_call(
        functools.partial(prep_kernel, members, rows),
        in_specs=[anywhere, anywhere],
        out_shape=[turned, turned, row, row],
        scratch_shapes=[columns_of, columns_of, pltpu.SemaphoreType.DMA((2, blocks))],
        name="prep",
        compiler_params=vmem_params(),
    )(flat_theta, flat_rho)

    above = lax.ppermute(down, "cell", along("cell", 1))
    below = lax.ppermute(top, "cell", along("cell", -1))
    rho1, down, top, part = pl.pallas_call(
        step1_kernel,
        out_shape=[turned, row, row, row],
        name="step1",
        compiler_params=vmem_params(),
    )(theta_t, rho_t, above, below)

    above = lax.ppermute(down, "cell", along("cell", 1))
    below = lax.ppermute(top, "cell", along("cell", -1))
    part = lax.ppermute(part, "cell", along("cell", -1))
    counts_shape = jax.ShapeDtypeStruct((members, sensors), F32)
    counts, rest = pl.pallas_call(
        step2_kernel,
        out_shape=[counts_shape, row],
        scratch_shapes=[pltpu.VMEM(((rows - 1) * blocks, members, LANES), F32)],
        name="step2",
        compiler_params=vmem_params(),
    )(theta_t, rho1, above, below, pos)
    own = pl.pallas_call(
        functools.partial(finish_kernel, (rows - 1) * blocks),
        out_shape=counts_shape,
        scratch_shapes=[pltpu.VMEM((blocks, members, LANES), F32)],
        name="finish",
        compiler_params=vmem_params(),
    )(rest, part, pos, counts)

    chip = lax.ppermute(own, "grp", swapped("grp", 2))
    core = lax.ppermute(own, "grp", swapped("grp", 1))
    both = lax.ppermute(chip, "grp", swapped("grp", 1))
    piece = pl.BlockSpec((members, sensors), lambda i, g: (0, 0))
    predicted, packed = pl.pallas_call(
        functools.partial(product_kernel, total),
        grid_spec=pltpu.PrefetchScalarGridSpec(
            num_scalar_prefetch=1,
            grid=(1,),
            in_specs=[piece] * 4
            + [
                pl.BlockSpec((members, sensors), lambda i, g: (g[0], 0)),
                pl.BlockSpec((1, sensors), lambda i, g: (0, 0)),
            ],
            out_specs=[
                pl.BlockSpec((total, sensors), lambda i, g: (0, 0)),
                pl.BlockSpec((total + members, total), lambda i, g: (0, 0)),
            ],
        ),
        out_shape=[
            jax.ShapeDtypeStruct((total, sensors), F32),
            jax.ShapeDtypeStruct((total + members, total), F32),
        ],
        name="product",
        compiler_params=vmem_params(),
    )(g, own, core, chip, both, perturbed, noise_var.reshape(1, sensors))

    bit = 1
    while bit < lax.axis_size("cell"):
        packed = packed + lax.ppermute(packed, "cell", swapped("cell", bit))
        bit *= 2
    system = (total - 1.0) * jnp.eye(total, dtype=F32) + packed[:total]
    factor = jnp.linalg.cholesky(system)
    mixing = jax.scipy.linalg.cho_solve((factor, True), packed[total:].T)
    mixing = mixing - jnp.mean(mixing, axis=0)

    chip_theta = lax.ppermute(flat_theta, "grp", swapped("grp", 2))
    core_theta = lax.ppermute(flat_theta, "grp", swapped("grp", 1))
    both_theta = lax.ppermute(chip_theta, "grp", swapped("grp", 1))
    new = pl.pallas_call(
        functools.partial(update_kernel, rows),
        in_specs=[pl.BlockSpec(memory_space=pltpu.SMEM), pl.BlockSpec(memory_space=pltpu.VMEM)] + [anywhere] * 4,
        out_specs=anywhere,
        out_shape=jax.ShapeDtypeStruct((members * rows, columns), F32),
        scratch_shapes=[
            pltpu.VMEM((4, blocks, members * rows, LANES), F32),
            columns_of,
            pltpu.SemaphoreType.DMA((4, blocks)),
            pltpu.SemaphoreType.DMA((blocks,)),
        ],
        name="update",
        compiler_params=vmem_params(),
    )(g, mixing, flat_theta, core_theta, chip_theta, both_theta)
    return (new.reshape(members, rows, columns), predicted)


def solution(mesh):
    return jax.shard_map(
        body,
        mesh=mesh,
        in_specs=(
            P("grp", "cell", None),
            P("grp", "cell", None),
            P("cell", None),
            P(None, "cell"),
            P("cell"),
        ),
        out_specs=(P("grp", "cell", None), P(None, "cell")),
        check_vma=False,
    )
```

```python
import functools

import jax
import jax.numpy as jnp
from jax import lax
from jax.experimental import pallas as pl
from jax.experimental.pallas import tpu as pltpu
from jax.sharding import PartitionSpec as P

LANES = 128
F32 = jnp.float32


def along(axis, shift):
    count = lax.axis_size(axis)
    return [(i, i + shift) for i in range(count) if 0 <= i + shift < count]


def swapped(axis, bit):
    return [(i, i ^ bit) for i in range(lax.axis_size(axis))]


def outflow(speed, rho):
    return 0.2 * (speed * rho * (1.0 - rho)) + 0.1 * rho


def from_left(x):
    lane = lax.broadcasted_iota(jnp.int32, x.shape, 1)
    return jnp.where(lane == 0, 0.0, pltpu.roll(x, 1, 1))


def from_right(x):
    last = x.shape[1] - 1
    lane = lax.broadcasted_iota(jnp.int32, x.shape, 1)
    return jnp.where(lane == last, 0.0, pltpu.roll(x, last, 1))


def without_above(rho, out, below):
    return 0.8 * rho - 2.0 * out + from_left(out) + 0.1 * (below + from_right(rho))


def box4(x):
    n = x.shape[1]
    pair = x + pltpu.roll(x, n - 1, 1)
    return pair + pltpu.roll(pair, n - 2, 1)


def load_columns(source, target, sems, first=0):
    copies = []
    for b in range(source.shape[1] // LANES):
        copy = pltpu.make_async_copy(
            source.at[:, pl.ds(b * LANES, LANES)], target.at[b, pl.ds(first, source.shape[0])], sems.at[b]
        )
        copy.start()
        copies.append(copy)
    return copies


def edge_kernel(rows, odd, theta, rho, low_pair, high_pair, theta_in, rho_in, sems):
    waits = load_columns(rho, rho_in, sems.at[0]), load_columns(theta, theta_in, sems.at[1])
    members = low_pair.shape[0]
    swap = odd[0] == 1
    for b in range(theta_in.shape[0]):
        at = slice(b * LANES, (b + 1) * LANES)
        waits[0][b].wait()
        waits[1][b].wait()
        last = pl.ds(rows - 1, members, stride=rows)
        down = outflow(theta_in[b, last, :], rho_in[b, last, :])
        top = rho_in[b, pl.ds(0, members, stride=rows), :]
        low_pair[:, at] = jnp.where(swap, top, down)
        high_pair[:, at] = jnp.where(swap, down, top)


def prep_kernel(members, rows, theta, rho, theta_t, rho_t, theta_in, rho_in, sems):
    waits = load_columns(rho, rho_in, sems.at[0]), load_columns(theta, theta_in, sems.at[1])
    for b in range(theta_in.shape[0]):
        at = slice(b * LANES, (b + 1) * LANES)
        waits[0][b].wait()
        waits[1][b].wait()
        for r in range(rows):
            theta_t[r, :, at] = theta_in[b, pl.ds(r, members, stride=rows), :]
            rho_t[r, :, at] = rho_in[b, pl.ds(r, members, stride=rows), :]


def step1_kernel(odd, theta, rho, from_low, from_high, rho1, low_pair, high_pair, part):
    rows, members, _ = rho.shape
    swap = odd[0] == 1

    def chunk(c, carry):
        at = pl.ds(c * 8, 8)
        low, high = from_low[at, :], from_high[at, :]
        up = jnp.where(swap, low, high)
        beneath = jnp.where(swap, high, low)
        kept = None
        for r in range(rows):
            now = rho[r, at, :]
            under = rho[r + 1, at, :] if r + 1 < rows else beneath
            speed = theta[r, at, :]
            out = outflow(speed, now)
            new = without_above(now, out, under) + up
            rho1[r, at, :] = new
            up = out
            if r == 0:
                kept = (new, outflow(speed, new))
            if r == 1:
                part[at, :] = without_above(kept[0], kept[1], new)
            if r == rows - 1:
                down = outflow(speed, new)
                low_pair[at, :] = jnp.where(swap, kept[0], down)
                high_pair[at, :] = jnp.where(swap, down, kept[0])
        return carry

    lax.fori_loop(0, members // 8, chunk, 0)


def pick(table, first, last, low, high, pos_ref, start, out_ref):
    members = out_ref.shape[0]
    parts = members // 8
    width = 4
    for g0 in range(0, pos_ref.shape[0], width):
        groups = range(g0, g0 + width)
        where = [jnp.broadcast_to(pos_ref[g : g + 1, :], (8, LANES)) for g in groups]
        lane = [w & (LANES - 1) for w in where]
        block = [w >> 7 for w in where]
        begin = [jnp.maximum(low[g], first) for g in groups]
        trips = functools.reduce(
            jnp.maximum, [jnp.minimum(high[g], last) + 1 - lo for g, lo in zip(groups, begin)]
        )
        init = tuple(
            start[i * 8 : i * 8 + 8, g * LANES : (g + 1) * LANES] if start is not None else jnp.zeros((8, LANES), F32)
            for g in groups
            for i in range(parts)
        )

        def look(t, acc):
            new = []
            for k in range(width):
                p = begin[k] + t
                at = jnp.minimum(p, last) - first
                hit = block[k] == p
                for i in range(parts):
                    row = table[at, i * 8 : i * 8 + 8, :]
                    got = jnp.take_along_axis(row, lane[k], axis=1, mode="promise_in_bounds")
                    new.append(jnp.where(hit, got, acc[k * parts + i]))
            return tuple(new)

        acc = lax.fori_loop(0, trips, look, init)
        for k, g in enumerate(groups):
            for i in range(parts):
                out_ref[i * 8 : i * 8 + 8, g * LANES : (g + 1) * LANES] = acc[k * parts + i]


def reorder_kernel(index, source, out):
    members = out.shape[0]
    groups = index.shape[0]

    def one(g, carry):
        where = jnp.broadcast_to(index[pl.ds(g, 1), :], (8, LANES))
        lane = where & (LANES - 1)
        block = where >> 7
        at = pl.ds(pl.multiple_of(g * LANES, LANES), LANES)
        for i in range(0, members, 8):
            acc = jnp.zeros((8, LANES), F32)
            for h in range(groups):
                row = source[i : i + 8, h * LANES : (h + 1) * LANES]
                got = jnp.take_along_axis(row, lane, axis=1, mode="promise_in_bounds")
                acc = jnp.where(block == h, got, acc)
            out[i : i + 8, at] = acc
        return carry

    lax.fori_loop(0, groups, one, 0)


def step2_kernel(odd, theta, rho, from_low, from_high, pos, low, high, counts, rest, table):
    rows, members, columns = rho.shape
    swap = odd[0] == 1
    blocks = columns // LANES

    def chunk(c, carry):
        at = pl.ds(c * 8, 8)
        first, second = from_low[at, :], from_high[at, :]
        up = jnp.where(swap, first, second)
        beneath = jnp.where(swap, second, first)
        last = None
        for r in range(rows):
            now = rho[r, at, :]
            under = rho[r + 1, at, :] if r + 1 < rows else beneath
            out = outflow(theta[r, at, :], now)
            new = without_above(now, out, under) + up
            up = out
            if r > 0:
                sums = box4(last + new)
                for b in range(blocks):
                    table[(r - 1) * blocks + b, at, :] = sums[:, b * LANES : (b + 1) * LANES]
            if r == rows - 1:
                rest[at, :] = new + out
            last = new
        return carry

    lax.fori_loop(0, members // 8, chunk, 0)
    pick(table, 0, (rows - 1) * blocks - 1, low, high, pos, None, counts)


def finish_kernel(first, rest, part, pos, low, high, counts, mine, table):
    members, columns = rest.shape
    blocks = columns // LANES
    for c in range(0, members, 8):
        sums = box4(rest[c : c + 8, :] + part[c : c + 8, :])
        for b in range(blocks):
            table[b, c : c + 8, :] = sums[:, b * LANES : (b + 1) * LANES]
    pick(table, first, first + blocks - 1, low, high, pos, counts, mine)


def product_kernel(total, g_ref, own, core, chip, both, perturbed, noise, packed, every):
    members, sensors = own.shape
    g = g_ref[0]
    for step, piece in enumerate((own, core, chip, both)):
        every[pl.ds(pl.multiple_of((g ^ step) * members, members), members), :] = piece[...]
    width = 512
    acc = None
    for s in range(0, sensors, width):
        at = slice(s, s + width)
        counts = every[:, at]
        anomaly = counts - jnp.sum(counts, axis=0, keepdims=True) / total
        weighted = anomaly / noise[:, at]
        left = jnp.concatenate([anomaly, perturbed[:, at] - own[:, at]], axis=0)
        term = lax.dot_general(
            left, weighted, (((1,), (1,)), ((), ())), precision=lax.Precision.HIGHEST, preferred_element_type=F32
        )
        acc = term if acc is None else acc + term
    packed[...] = acc


def bcast_lane(x, k):
    return jnp.broadcast_to(x[:, k : k + 1], x.shape)


def solve_kernel(shift, packed, mixing_t):
    n = packed.shape[1]
    lane = lax.broadcasted_iota(jnp.int32, (8, n), 1)
    sub = lax.broadcasted_iota(jnp.int32, (8, n), 0)
    a = []
    for i in range(packed.shape[0] // 8):
        x = packed[i * 8 : i * 8 + 8, :]
        a.append(jnp.where(lane == sub + i * 8, x + shift, x) if i * 8 < n else x)
    keep = jnp.zeros((8, n), F32)
    mix = jnp.zeros((8, n), F32)
    for k in range(0, n, 2):
        r = k % 8
        top = a[k // 8]
        r0 = jnp.broadcast_to(top[r : r + 1, :], (8, n))
        r1 = jnp.broadcast_to(top[r + 1 : r + 2, :], (8, n))
        p00, p01, p10, p11 = bcast_lane(r0, k), bcast_lane(r0, k + 1), bcast_lane(r1, k), bcast_lane(r1, k + 1)
        scale = 1.0 / (p00 * p11 - p01 * p10)
        here = (lane == k) | (lane == k + 1)
        f0 = jnp.where(here, 0.0, scale * (p11 * r0 - p01 * r1))
        f1 = jnp.where(here, 0.0, scale * (p00 * r1 - p10 * r0))
        keep = jnp.where(lane == k, scale * p11, jnp.where(lane == k + 1, scale * p00, keep))
        mix = jnp.where(lane == k, -(scale * p10), jnp.where(lane == k + 1, -(scale * p01), mix))
        for i in range(k // 8, len(a)):
            a[i] = a[i] - (bcast_lane(a[i], k) * f0 + bcast_lane(a[i], k + 1) * f1)
    even = (lane & 1) == 0
    for i in range(n // 8, len(a)):
        x = a[i]
        other = jnp.where(even, pltpu.roll(x, n - 1, 1), pltpu.roll(x, 1, 1))
        w = x * keep + other * mix
        w = w - jnp.sum(w, axis=1, keepdims=True) / n
        at = i * 8 - n
        mixing_t[at : at + 8, :] = w


def split(x):
    high = x.astype(jnp.bfloat16)
    return high, (x - high.astype(F32)).astype(jnp.bfloat16)


def update_kernel(rows, g_ref, mixing, own, core, chip, both, chip2, both2, out, fields, new, sems, out_sems):
    members = own.shape[0] // rows
    g = g_ref[0]
    cut = chip.shape[0]
    places = ((own, 0, 0), (core, 1, 0), (chip, 2, 0), (chip2, 2, cut), (both, 3, 0), (both2, 3, cut))
    waits = [load_columns(piece, fields.at[k], sems.at[i], first) for i, (piece, k, first) in enumerate(places)]
    wt = mixing[...]
    n = wt.shape[1]
    lane = lax.broadcasted_iota(jnp.int32, wt.shape, 1)
    crossed = jnp.where((lane & members) == 0, pltpu.roll(wt, n - members, 1), pltpu.roll(wt, members, 1))
    wt = jnp.where((g & 1) == 1, crossed, wt)
    wt = jnp.where((g & 2) == 2, pltpu.roll(wt, n // 2, 1), wt)
    wh, wl = split(wt)
    sent = []
    for b in range(new.shape[0]):
        for wait in waits:
            wait[b].wait()
        for r in range(rows):
            at = pl.ds(r, members, stride=rows)
            x = [fields[k, b, at, :] for k in range(4)]
            xh, xl = split(jnp.concatenate(x, axis=0))
            add = (
                jnp.dot(wh, xh, preferred_element_type=F32)
                + jnp.dot(wh, xl, preferred_element_type=F32)
                + jnp.dot(wl, xh, preferred_element_type=F32)
            )
            new[b, at, :] = x[0] + add
        copy = pltpu.make_async_copy(new.at[b], out.at[:, pl.ds(b * LANES, LANES)], out_sems.at[b])
        copy.start()
        sent.append(copy)
    for copy in sent:
        copy.wait()


def tie(*values):
    return lax.optimization_barrier(values)


def kernel_params(mib):
    return pltpu.CompilerParams(vmem_limit_bytes=mib * 1024 * 1024)


def body(theta, density, footprint, perturbed, noise_var):
    members, rows, columns = theta.shape
    total = members * lax.axis_size("grp")
    sensors = footprint.shape[0]
    slab = rows * columns
    blocks = columns // LANES
    groups = sensors // LANES
    flat_theta = theta.reshape(members * rows, columns)
    flat_rho = density.reshape(members * rows, columns)
    g = lax.axis_index("grp").astype(jnp.int32).reshape(1)
    row = jax.ShapeDtypeStruct((members, columns), F32)
    turned = jax.ShapeDtypeStruct((rows, members, columns), F32)
    counts_shape = jax.ShapeDtypeStruct((members, sensors), F32)
    anywhere = pl.BlockSpec(memory_space=pltpu.HBM)
    vmem = pl.BlockSpec(memory_space=pltpu.VMEM)
    smem = pl.BlockSpec(memory_space=pltpu.SMEM)
    columns_of = pltpu.VMEM((blocks, members * rows, LANES), F32)

    odd = (lax.axis_index("cell") & 1).astype(jnp.int32).reshape(1)
    count = lax.axis_size("cell")
    far = [(i, i + 1 if i & 1 else i - 1) for i in range(1, count - 1)]

    def both_ways(low_pair, high_pair):
        from_high = lax.ppermute(high_pair, "cell", far)
        return lax.ppermute(low_pair, "cell", swapped("cell", 1)), from_high

    down, top = pl.pallas_call(
        functools.partial(edge_kernel, rows),
        in_specs=[smem, anywhere, anywhere],
        out_shape=[row, row],
        scratch_shapes=[columns_of, columns_of, pltpu.SemaphoreType.DMA((2, blocks))],
        name="edge",
        compiler_params=kernel_params(60),
    )(odd, flat_theta, flat_rho)
    above, below = both_ways(down, top)
    cut = members // 2 * rows
    chip_theta = lax.ppermute(flat_theta[:cut], "grp", swapped("grp", 2))

    down, flat_theta, flat_rho, first = tie(down, flat_theta, flat_rho, footprint[:, 0])
    theta_t, rho_t = pl.pallas_call(
        functools.partial(prep_kernel, members, rows),
        in_specs=[anywhere, anywhere],
        out_shape=[turned, turned],
        scratch_shapes=[columns_of, columns_of, pltpu.SemaphoreType.DMA((2, blocks))],
        name="prep",
        compiler_params=kernel_params(12),
    )(flat_theta, flat_rho)
    key = (first - lax.axis_index("cell") * slab) * sensors + lax.iota(jnp.int32, sensors)
    rank = jnp.sum((key[:, None] < key[None, :]).astype(jnp.int32), axis=0)
    chosen = rank[:, None] == lax.iota(jnp.int32, sensors)[None, :]
    ordered = jnp.sum(jnp.where(chosen, key[:, None], 0), axis=0)
    above, below, ordered, rank = tie(above, below, ordered, rank)

    rho1, down, top, part = pl.pallas_call(
        step1_kernel,
        in_specs=[smem] + [vmem] * 4,
        out_shape=[turned, row, row, row],
        name="step1",
        compiler_params=kernel_params(12),
    )(odd, theta_t, rho_t, above, below)
    above, below = both_ways(down, top)
    part = lax.ppermute(part, "cell", along("cell", -1))

    down, rank, ordered, noise_var, perturbed = tie(down, rank, ordered, noise_var, perturbed)
    chosen = rank[:, None] == lax.iota(jnp.int32, sensors)[None, :]
    noise = jnp.sum(jnp.where(chosen, noise_var[:, None], 0.0), axis=0).reshape(1, sensors)
    pos = (ordered // sensors).reshape(groups, LANES)
    order = (ordered & (sensors - 1)).reshape(groups, LANES)
    rank = rank.reshape(groups, LANES)
    low = pos[:, 0] >> 7
    high = pos[:, LANES - 1] >> 7
    perturbed_own = pl.pallas_call(
        lambda g, index, source, out: reorder_kernel(index, source, out),
        grid_spec=pltpu.PrefetchScalarGridSpec(
            num_scalar_prefetch=1,
            grid=(1,),
            in_specs=[
                pl.BlockSpec((groups, LANES), lambda i, g: (0, 0)),
                pl.BlockSpec((members, sensors), lambda i, g: (g[0], 0)),
            ],
            out_specs=pl.BlockSpec((members, sensors), lambda i, g: (0, 0)),
        ),
        out_shape=counts_shape,
        name="reorder",
        compiler_params=kernel_params(4),
    )(g, order, perturbed)
    above, below, noise, perturbed_own, pos, low, high, rank = tie(
        above, below, noise, perturbed_own, pos, low, high, rank
    )

    counts, rest = pl.pallas_call(
        step2_kernel,
        in_specs=[smem] + [vmem] * 5 + [smem] * 2,
        out_shape=[counts_shape, row],
        scratch_shapes=[pltpu.VMEM(((rows - 1) * blocks, members, LANES), F32)],
        name="step2",
        compiler_params=kernel_params(12),
    )(odd, theta_t, rho1, above, below, pos, low, high)
    rest, part = tie(rest, part)
    own = pl.pallas_call(
        functools.partial(finish_kernel, (rows - 1) * blocks),
        in_specs=[vmem] * 3 + [smem] * 2 + [vmem],
        out_shape=counts_shape,
        scratch_shapes=[pltpu.VMEM((blocks, members, LANES), F32)],
        name="finish",
        compiler_params=kernel_params(4),
    )(rest, part, pos, low, high, counts)

    chip = lax.ppermute(own, "grp", swapped("grp", 2))
    core = lax.ppermute(own, "grp", swapped("grp", 1))
    both = lax.ppermute(chip, "grp", swapped("grp", 1))
    mine = pl.pallas_call(
        reorder_kernel, out_shape=counts_shape, name="restore", compiler_params=kernel_params(4)
    )(rank, own)
    rest = flat_theta[cut:]
    chip, core, mine, rest, chip_theta = tie(chip, core, mine, rest, chip_theta)
    chip_rest = lax.ppermute(rest, "grp", swapped("grp", 2))
    both_theta = lax.ppermute(chip_theta, "grp", swapped("grp", 1))
    packed = pl.pallas_call(
        functools.partial(product_kernel, total),
        in_specs=[smem] + [vmem] * 6,
        out_shape=jax.ShapeDtypeStruct((total + members, total), F32),
        scratch_shapes=[pltpu.VMEM((total, sensors), F32)],
        name="product",
        compiler_params=kernel_params(12),
    )(g, own, core, chip, both, perturbed_own, noise)

    flat_theta, packed = tie(flat_theta, packed)

    def restore(counts):
        return pl.pallas_call(
            reorder_kernel, out_shape=counts_shape, name="restore", compiler_params=kernel_params(4)
        )(rank, counts)

    def assemble(g_ref, own, core, chip, both, out):
        g = g_ref[0]
        for step, piece in enumerate((own, core, chip, both)):
            out[pl.ds(pl.multiple_of((g ^ step) * members, members), members), :] = piece[...]

    core_theta = lax.ppermute(flat_theta, "grp", swapped("grp", 1))
    for stage, bit in enumerate((1, 2, 8, 16, 4)):
        other = lax.ppermute(packed, "cell", swapped("cell", bit))
        if stage == 0:
            core, packed = tie(core, packed)
            core = restore(core)
            other, core = tie(other, core)
        if stage == 1:
            chip, packed = tie(chip, packed)
            chip = restore(chip)
            other, chip = tie(other, chip)
        if stage == 2:
            both, packed = tie(both, packed)
            both = restore(both)
            other, both = tie(other, both)
        if stage == 4:
            both_rest = lax.ppermute(chip_rest, "grp", swapped("grp", 1))
            predicted = pl.pallas_call(
                assemble,
                in_specs=[smem] + [vmem] * 4,
                out_shape=jax.ShapeDtypeStruct((total, sensors), F32),
                name="assemble",
                compiler_params=kernel_params(4),
            )(g, mine, core, chip, both)
            other, predicted = tie(other, predicted)
        packed = packed + other
        if stage == 3:
            packed, chip_rest = tie(packed, chip_rest)
    mixing_t = pl.pallas_call(
        functools.partial(solve_kernel, total - 1.0),
        out_shape=jax.ShapeDtypeStruct((members, total), F32),
        name="solve",
        compiler_params=kernel_params(4),
    )(packed)
    new = pl.pallas_call(
        functools.partial(update_kernel, rows),
        in_specs=[smem, vmem] + [anywhere] * 6,
        out_specs=anywhere,
        out_shape=jax.ShapeDtypeStruct((members * rows, columns), F32),
        scratch_shapes=[
            pltpu.VMEM((4, blocks, members * rows, LANES), F32),
            columns_of,
            pltpu.SemaphoreType.DMA((6, blocks)),
            pltpu.SemaphoreType.DMA((blocks,)),
        ],
        name="update",
        compiler_params=kernel_params(16),
    )(g, mixing_t, flat_theta, core_theta, chip_theta, both_theta, chip_rest, both_rest)
    return (new.reshape(members, rows, columns), predicted)


def solution(mesh):
    return jax.shard_map(
        body,
        mesh=mesh,
        in_specs=(
            P("grp", "cell", None),
            P("grp", "cell", None),
            P("cell", None),
            P(None, "cell"),
            P("cell"),
        ),
        out_specs=(P("grp", "cell", None), P(None, "cell")),
        check_vma=False,
    )
```

```python
import functools

import jax
import jax.numpy as jnp
from jax import lax
from jax.experimental import pallas as pl
from jax.experimental.pallas import tpu as pltpu
from jax.sharding import PartitionSpec as P

LANES = 128
F32 = jnp.float32


def along(axis, shift):
    count = lax.axis_size(axis)
    return [(i, i + shift) for i in range(count) if 0 <= i + shift < count]


def swapped(axis, bit):
    return [(i, i ^ bit) for i in range(lax.axis_size(axis))]


def outflow(speed, rho):
    return 0.2 * (speed * rho * (1.0 - rho)) + 0.1 * rho


def from_left(x):
    lane = lax.broadcasted_iota(jnp.int32, x.shape, 1)
    return jnp.where(lane == 0, 0.0, pltpu.roll(x, 1, 1))


def from_right(x):
    last = x.shape[1] - 1
    lane = lax.broadcasted_iota(jnp.int32, x.shape, 1)
    return jnp.where(lane == last, 0.0, pltpu.roll(x, last, 1))


def without_above(rho, out, below):
    return 0.8 * rho - 2.0 * out + from_left(out) + 0.1 * (below + from_right(rho))


def box4(x):
    n = x.shape[1]
    pair = x + pltpu.roll(x, n - 1, 1)
    return pair + pltpu.roll(pair, n - 2, 1)


def load_columns(source, target, sems):
    copies = []
    for b in range(source.shape[1] // LANES):
        copy = pltpu.make_async_copy(source.at[:, pl.ds(b * LANES, LANES)], target.at[b], sems.at[b])
        copy.start()
        copies.append(copy)
    return copies


def prep_kernel(rows, odd, theta, rho, low_pair, high_pair, theta_a, theta_b, theta_in, rho_in, sems):
    waits = load_columns(rho, rho_in, sems.at[0]), load_columns(theta, theta_in, sems.at[1])
    members = low_pair.shape[0]
    half = theta_a.shape[0]
    swap = odd[0] == 1
    for b in range(theta_in.shape[0]):
        at = slice(b * LANES, (b + 1) * LANES)
        waits[0][b].wait()
        waits[1][b].wait()
        speed = [theta_in[b, pl.ds(r, members, stride=rows), :] for r in range(rows)]
        first, last = (rho_in[b, pl.ds(r, members, stride=rows), :] for r in (0, rows - 1))
        for r in range(rows):
            if r < half:
                theta_a[r, :, at] = speed[r]
            else:
                theta_b[r - half, :, at] = speed[r]
        down = outflow(speed[-1], last)
        low_pair[:, at] = jnp.where(swap, first, down)
        high_pair[:, at] = jnp.where(swap, down, first)


def rows_of(theta_a, theta_b, at):
    return [ref[r, at, :] for ref in (theta_a, theta_b) for r in range(ref.shape[0])]


def advance(speed, rho):
    out = [outflow(s, x) for s, x in zip(speed, rho)]
    new = []
    for r, x in enumerate(rho):
        under = rho[r + 1] + from_right(x) if r + 1 < len(rho) else from_right(x)
        y = 0.8 * x - 2.0 * out[r] + from_left(out[r]) + 0.1 * under
        new.append(y + out[r - 1] if r else y)
    return new, out


def inner1_kernel(theta_a, theta_b, rho, rho1, rho_in, sems):
    rows, members, _ = rho1.shape
    for b, copy in enumerate(load_columns(rho, rho_in, sems)):
        copy.wait()
        for r in range(rows):
            rho1[r, :, b * LANES : (b + 1) * LANES] = rho_in[b, pl.ds(r, members, stride=rows), :]

    def chunk(c, carry):
        at = pl.ds(c * 8, 8)
        new, _ = advance(rows_of(theta_a, theta_b, at), [rho1[r, at, :] for r in range(rows)])
        for r in range(rows):
            rho1[r, at, :] = new[r]
        return carry

    lax.fori_loop(0, members // 8, chunk, 0)


def edge1_kernel(odd, theta_a, theta_b, rho1, from_low, from_high, low_pair, high_pair, part, first, last):
    rows, members, _ = rho1.shape
    swap = odd[0] == 1

    def chunk(c, carry):
        at = pl.ds(c * 8, 8)
        low, high = from_low[at, :], from_high[at, :]
        top = rho1[0, at, :] + jnp.where(swap, low, high)
        bottom = rho1[rows - 1, at, :] + 0.1 * jnp.where(swap, high, low)
        down = outflow(theta_b[theta_b.shape[0] - 1, at, :], bottom)
        low_pair[at, :] = jnp.where(swap, top, down)
        high_pair[at, :] = jnp.where(swap, down, top)
        part[at, :] = without_above(top, outflow(theta_a[0, at, :], top), rho1[1, at, :])
        first[at, :] = top
        last[at, :] = bottom
        return carry

    lax.fori_loop(0, members // 8, chunk, 0)


def pick(table, first, last, low, high, pos_ref, start, out_ref):
    members = out_ref.shape[0]
    parts = members // 8
    width = 4
    for g0 in range(0, pos_ref.shape[0], width):
        groups = range(g0, g0 + width)
        where = [jnp.broadcast_to(pos_ref[g : g + 1, :], (8, LANES)) for g in groups]
        lane = [w & (LANES - 1) for w in where]
        block = [w >> 7 for w in where]
        begin = [jnp.maximum(low[g], first) for g in groups]
        trips = functools.reduce(
            jnp.maximum, [jnp.minimum(high[g], last) + 1 - lo for g, lo in zip(groups, begin)]
        )
        init = tuple(
            start[i * 8 : i * 8 + 8, g * LANES : (g + 1) * LANES] if start is not None else jnp.zeros((8, LANES), F32)
            for g in groups
            for i in range(parts)
        )

        def look(t, acc):
            new = []
            for k in range(width):
                p = begin[k] + t
                at = jnp.minimum(p, last) - first
                hit = block[k] == jnp.where(p <= last, p, -1)
                for i in range(parts):
                    row = table[at, i * 8 : i * 8 + 8, :]
                    got = jnp.take_along_axis(row, lane[k], axis=1, mode="promise_in_bounds")
                    new.append(jnp.where(hit, got, acc[k * parts + i]))
            return tuple(new)

        acc = lax.fori_loop(0, trips, look, init)
        for k, g in enumerate(groups):
            for i in range(parts):
                out_ref[i * 8 : i * 8 + 8, g * LANES : (g + 1) * LANES] = acc[k * parts + i]


def reorder_kernel(index, source, out, extra=None, extra_out=None):
    members = out.shape[0]
    groups = index.shape[0]

    def one(g, carry):
        where = jnp.broadcast_to(index[pl.ds(g, 1), :], (8, LANES))
        lane = where & (LANES - 1)
        block = where >> 7
        at = pl.ds(pl.multiple_of(g * LANES, LANES), LANES)
        for i in range(0, members, 8):
            acc = jnp.zeros((8, LANES), F32)
            for h in range(groups):
                row = source[i : i + 8, h * LANES : (h + 1) * LANES]
                got = jnp.take_along_axis(row, lane, axis=1, mode="promise_in_bounds")
                acc = jnp.where(block == h, got, acc)
            out[i : i + 8, at] = acc
        if extra is not None:
            acc = jnp.zeros((8, LANES), F32)
            for h in range(groups):
                row = jnp.broadcast_to(extra[:, h * LANES : (h + 1) * LANES], (8, LANES))
                got = jnp.take_along_axis(row, lane, axis=1, mode="promise_in_bounds")
                acc = jnp.where(block == h, got, acc)
            extra_out[:, at] = acc[:1]
        return carry

    lax.fori_loop(0, groups, one, 0)


def store_sums(table, row, at, x):
    sums = box4(x)
    blocks = x.shape[1] // LANES
    for b in range(blocks):
        table[row * blocks + b, at, :] = sums[:, b * LANES : (b + 1) * LANES]


def inner2_kernel(theta_a, theta_b, rho, first, last, pos, low, high, counts, head, tail, rest, table):
    rows, members, columns = rho.shape
    blocks = columns // LANES

    def chunk(c, carry):
        at = pl.ds(c * 8, 8)
        now = [first[at, :]] + [rho[r, at, :] for r in range(1, rows - 1)] + [last[at, :]]
        new, out = advance(rows_of(theta_a, theta_b, at), now)
        head[at, :] = new[0] + new[1]
        tail[at, :] = new[rows - 2] + new[rows - 1]
        rest[at, :] = new[rows - 1] + out[rows - 1]
        for r in range(1, rows - 2):
            store_sums(table, r - 1, at, new[r] + new[r + 1])
        return carry

    lax.fori_loop(0, members // 8, chunk, 0)
    pick(table, blocks, (rows - 2) * blocks - 1, low, high, pos, None, counts)


def edge2_kernel(rows, odd, head, tail, from_low, from_high, pos, low, high, counts, more, table):
    members, columns = head.shape
    blocks = columns // LANES
    swap = odd[0] == 1
    for c in range(0, members, 8):
        at = pl.ds(c, 8)
        one, two = from_low[at, :], from_high[at, :]
        store_sums(table, 0, at, head[at, :] + jnp.where(swap, one, two))
        store_sums(table, 1, at, tail[at, :] + 0.1 * jnp.where(swap, two, one))
    pick(table, 0, blocks - 1, low, high, pos, counts, more)
    pick(table.at[pl.ds(blocks, blocks)], (rows - 2) * blocks, (rows - 1) * blocks - 1, low, high, pos, more, more)


def finish_kernel(first, odd, rest, from_low, from_high, part, pos, low, high, counts, mine, table):
    members, columns = rest.shape
    blocks = columns // LANES
    swap = odd[0] == 1
    for c in range(0, members, 8):
        at = pl.ds(c, 8)
        beneath = jnp.where(swap, from_high[at, :], from_low[at, :])
        store_sums(table, 0, at, rest[at, :] + 0.1 * beneath + part[at, :])
    pick(table, first, first + blocks - 1, low, high, pos, counts, mine)


def product_kernel(total, g_ref, own, core, chip, both, perturbed, noise, packed, every):
    members, sensors = own.shape
    g = g_ref[0]
    for step, piece in enumerate((own, core, chip, both)):
        every[pl.ds(pl.multiple_of((g ^ step) * members, members), members), :] = piece[...]
    width = 512
    acc = None
    for s in range(0, sensors, width):
        at = slice(s, s + width)
        counts = every[:, at]
        anomaly = counts - jnp.sum(counts, axis=0, keepdims=True) / total
        weighted = anomaly / noise[:, at]
        left = jnp.concatenate([anomaly, perturbed[:, at] - own[:, at]], axis=0)
        term = lax.dot_general(
            left, weighted, (((1,), (1,)), ((), ())), precision=lax.Precision.HIGHEST, preferred_element_type=F32
        )
        acc = term if acc is None else acc + term
    packed[...] = acc


def lane_of(x, k):
    return jnp.take_along_axis(x, jnp.full(x.shape, k, jnp.int32), axis=1, mode="promise_in_bounds")


def sublane_of(x, r):
    return jnp.broadcast_to(x[r : r + 1, :], x.shape)


def solve_kernel(shift, packed, mixing_t):
    n = packed.shape[1]
    lane = lax.broadcasted_iota(jnp.int32, (8, n), 1)
    sub = lax.broadcasted_iota(jnp.int32, (8, n), 0)
    a = []
    for i in range(packed.shape[0] // 8):
        x = packed[i * 8 : i * 8 + 8, :]
        a.append(jnp.where(lane == sub + i * 8, x + shift, x) if i * 8 < n else x)
    keep = jnp.zeros((8, n), F32)
    mix = jnp.zeros((8, n), F32)
    for k in range(0, n, 2):
        r = k % 8
        top = a[k // 8]
        c0, c1 = lane_of(top, k), lane_of(top, k + 1)
        r0, r1 = sublane_of(top, r), sublane_of(top, r + 1)
        p00, p01, p10, p11 = sublane_of(c0, r), sublane_of(c1, r), sublane_of(c0, r + 1), sublane_of(c1, r + 1)
        scale = 1.0 / (p00 * p11 - p01 * p10)
        here = (lane == k) | (lane == k + 1)
        f0 = jnp.where(here, 0.0, scale * (p11 * r0 - p01 * r1))
        f1 = jnp.where(here, 0.0, scale * (p00 * r1 - p10 * r0))
        keep = jnp.where(lane == k, scale * p11, jnp.where(lane == k + 1, scale * p00, keep))
        mix = jnp.where(lane == k, -(scale * p10), jnp.where(lane == k + 1, -(scale * p01), mix))
        for i in range(k // 8, len(a)):
            if i > k // 8:
                c0, c1 = lane_of(a[i], k), lane_of(a[i], k + 1)
            a[i] = a[i] - (c0 * f0 + c1 * f1)
    even = (lane & 1) == 0
    for i in range(n // 8, len(a)):
        x = a[i]
        other = jnp.where(even, pltpu.roll(x, n - 1, 1), pltpu.roll(x, 1, 1))
        w = x * keep + other * mix
        w = w - jnp.sum(w, axis=1, keepdims=True) / n
        at = i * 8 - n
        mixing_t[at : at + 8, :] = w


def split(x):
    high = x.astype(jnp.bfloat16)
    return high, (x - high.astype(F32)).astype(jnp.bfloat16)


def update_kernel(g_ref, mixing, *refs):
    pieces, (out, new, sems) = (refs[:4], refs[4:8]), refs[8:]
    half, members, columns = pieces[0][0].shape
    rows = half + pieces[1][0].shape[0]
    g = g_ref[0]
    wt = mixing[...]
    n = wt.shape[1]
    lane = lax.broadcasted_iota(jnp.int32, wt.shape, 1)
    crossed = jnp.where((lane & members) == 0, pltpu.roll(wt, n - members, 1), pltpu.roll(wt, members, 1))
    wt = jnp.where((g & 1) == 1, crossed, wt)
    wt = jnp.where((g & 2) == 2, pltpu.roll(wt, n // 2, 1), wt)
    wh, wl = split(wt)
    both = jnp.concatenate([wh, wl], axis=0)
    width = 2 * LANES
    sent = []
    for c in range(0, columns, width):
        for r in range(rows):
            x = [piece[r % half if r < half else r - half, :, c : c + width] for piece in pieces[r >= half]]
            xh, xl = split(jnp.concatenate(x, axis=0))
            high = jnp.dot(both, xh, preferred_element_type=F32)
            y = x[0] + (high[:members] + high[members:] + jnp.dot(wh, xl, preferred_element_type=F32))
            for k in range(width // LANES):
                new[c // LANES + k, pl.ds(r, members, stride=rows), :] = y[:, k * LANES : (k + 1) * LANES]
        for b in range(c // LANES, (c + width) // LANES):
            copy = pltpu.make_async_copy(new.at[b], out.at[:, pl.ds(b * LANES, LANES)], sems.at[b])
            copy.start()
            sent.append(copy)
    for copy in sent:
        copy.wait()


def tie(*values):
    return lax.optimization_barrier(values)


def kernel_params(mib):
    return pltpu.CompilerParams(vmem_limit_bytes=mib * 1024 * 1024)


def body(theta, density, footprint, perturbed, noise_var):
    members, rows, columns = theta.shape
    total = members * lax.axis_size("grp")
    sensors = footprint.shape[0]
    slab = rows * columns
    blocks = columns // LANES
    groups = sensors // LANES
    flat_theta = theta.reshape(members * rows, columns)
    flat_rho = density.reshape(members * rows, columns)
    g = lax.axis_index("grp").astype(jnp.int32).reshape(1)
    row = jax.ShapeDtypeStruct((members, columns), F32)
    turned = jax.ShapeDtypeStruct((rows, members, columns), F32)
    counts_shape = jax.ShapeDtypeStruct((members, sensors), F32)
    anywhere = pl.BlockSpec(memory_space=pltpu.HBM)
    vmem = pl.BlockSpec(memory_space=pltpu.VMEM)
    smem = pl.BlockSpec(memory_space=pltpu.SMEM)
    columns_of = pltpu.VMEM((blocks, members * rows, LANES), F32)

    odd = (lax.axis_index("cell") & 1).astype(jnp.int32).reshape(1)
    count = lax.axis_size("cell")
    far = [(i, i + 1 if i & 1 else i - 1) for i in range(1, count - 1)]

    def both_ways(low_pair, high_pair):
        from_low = lax.ppermute(low_pair, "cell", swapped("cell", 1))
        from_high = lax.ppermute(high_pair, "cell", far)
        return from_low, from_high

    early, late = (jax.ShapeDtypeStruct((n, members, columns), F32) for n in (rows * 3 // 8, rows - rows * 3 // 8))
    down, top, theta_a, theta_b = pl.pallas_call(
        functools.partial(prep_kernel, rows),
        in_specs=[smem, anywhere, anywhere],
        out_shape=[row, row, early, late],
        scratch_shapes=[columns_of, columns_of, pltpu.SemaphoreType.DMA((2, blocks))],
        name="prep",
        compiler_params=kernel_params(16),
    )(odd, flat_theta, flat_rho)
    above, below = both_ways(down, top)
    chip_a = lax.ppermute(theta_a, "grp", swapped("grp", 2))

    first = footprint[:, 0]
    rho1 = pl.pallas_call(
        inner1_kernel,
        in_specs=[vmem, vmem, anywhere],
        out_shape=turned,
        scratch_shapes=[columns_of, pltpu.SemaphoreType.DMA((blocks,))],
        name="inner1",
        compiler_params=kernel_params(12),
    )(theta_a, theta_b, flat_rho)
    rho1, first = tie(rho1, first)
    key = (first - lax.axis_index("cell") * slab) * sensors + lax.iota(jnp.int32, sensors)
    rank = jnp.sum((key[:, None] < key[None, :]).astype(jnp.int32), axis=0)
    chosen = rank[:, None] == lax.iota(jnp.int32, sensors)[None, :]
    ordered = jnp.sum(jnp.where(chosen, key[:, None], 0), axis=0)
    pos = (ordered // sensors).reshape(groups, LANES)
    order = (ordered & (sensors - 1)).reshape(groups, LANES)
    rank = rank.reshape(groups, LANES)
    low = pos[:, 0] >> 7
    high = pos[:, LANES - 1] >> 7
    above, below, pos, order, low, high, rank, rho1 = tie(above, below, pos, order, low, high, rank, rho1)

    low_pair, high_pair, part, first, last = pl.pallas_call(
        edge1_kernel,
        in_specs=[smem] + [vmem] * 5,
        out_shape=[row] * 5,
        name="edge1",
        compiler_params=kernel_params(12),
    )(odd, theta_a, theta_b, rho1, above, below)
    above, below = both_ways(low_pair, high_pair)
    part = lax.ppermute(part, "cell", along("cell", -1))

    counts, head, tail, rest = pl.pallas_call(
        inner2_kernel,
        in_specs=[vmem] * 6 + [smem] * 2,
        out_shape=[counts_shape, row, row, row],
        scratch_shapes=[pltpu.VMEM(((rows - 3) * blocks, members, LANES), F32)],
        name="inner2",
        compiler_params=kernel_params(14),
    )(theta_a, theta_b, rho1, first, last, pos, low, high)
    above, below, counts, head, tail, rest = tie(above, below, counts, head, tail, rest)
    counts = pl.pallas_call(
        functools.partial(edge2_kernel, rows),
        in_specs=[smem] + [vmem] * 5 + [smem] * 2 + [vmem],
        out_shape=counts_shape,
        scratch_shapes=[pltpu.VMEM((2 * blocks, members, LANES), F32)],
        name="edge2",
        compiler_params=kernel_params(6),
    )(odd, head, tail, above, below, pos, low, high, counts)
    counts, part = tie(counts, part)
    own = pl.pallas_call(
        functools.partial(finish_kernel, (rows - 1) * blocks),
        in_specs=[smem] + [vmem] * 5 + [smem] * 2 + [vmem],
        out_shape=counts_shape,
        scratch_shapes=[pltpu.VMEM((blocks, members, LANES), F32)],
        name="finish",
        compiler_params=kernel_params(6),
    )(odd, rest, above, below, part, pos, low, high, counts)

    def restore(counts):
        return pl.pallas_call(
            reorder_kernel, out_shape=counts_shape, name="restore", compiler_params=kernel_params(4)
        )(rank, counts)

    chip = lax.ppermute(own, "grp", swapped("grp", 2))
    core = lax.ppermute(own, "grp", swapped("grp", 1))
    own, perturbed = tie(own, perturbed)
    perturbed_own, noise = pl.pallas_call(
        lambda g, index, source, extra, out, extra_out: reorder_kernel(index, source, out, extra, extra_out),
        grid_spec=pltpu.PrefetchScalarGridSpec(
            num_scalar_prefetch=1,
            grid=(1,),
            in_specs=[
                pl.BlockSpec((groups, LANES), lambda i, g: (0, 0)),
                pl.BlockSpec((members, sensors), lambda i, g: (g[0], 0)),
                pl.BlockSpec((1, sensors), lambda i, g: (0, 0)),
            ],
            out_specs=[
                pl.BlockSpec((members, sensors), lambda i, g: (0, 0)),
                pl.BlockSpec((1, sensors), lambda i, g: (0, 0)),
            ],
        ),
        out_shape=[counts_shape, jax.ShapeDtypeStruct((1, sensors), F32)],
        name="reorder",
        compiler_params=kernel_params(4),
    )(g, order, perturbed, noise_var.reshape(1, sensors))
    chip, perturbed_own = tie(chip, perturbed_own)
    both = lax.ppermute(chip, "grp", swapped("grp", 1))
    core, both, chip_a, theta_b = tie(core, both, chip_a, theta_b)
    chip_b = lax.ppermute(theta_b, "grp", swapped("grp", 2))
    both_a = lax.ppermute(chip_a, "grp", swapped("grp", 1))
    packed = pl.pallas_call(
        functools.partial(product_kernel, total),
        in_specs=[smem] + [vmem] * 6,
        out_shape=jax.ShapeDtypeStruct((total + members, total), F32),
        scratch_shapes=[pltpu.VMEM((total, sensors), F32)],
        name="product",
        compiler_params=kernel_params(12),
    )(g, own, core, chip, both, perturbed_own, noise)

    theta_a, packed = tie(theta_a, packed)

    def assemble(g_ref, own, core, chip, both, out):
        g = g_ref[0]
        for step, piece in enumerate((own, core, chip, both)):
            out[pl.ds(pl.multiple_of((g ^ step) * members, members), members), :] = piece[...]

    core_a = lax.ppermute(theta_a, "grp", swapped("grp", 1))
    core_b = lax.ppermute(theta_b, "grp", swapped("grp", 1))
    for stage, bit in enumerate((1, 2, 8, 16, 4)):
        other = lax.ppermute(packed, "cell", swapped("cell", bit))
        if stage == 0:
            core, packed = tie(core, packed)
            core = restore(core)
            other, core = tie(other, core)
        if stage == 1:
            chip, packed = tie(chip, packed)
            chip = restore(chip)
            other, chip = tie(other, chip)
        if stage == 2:
            both, packed = tie(both, packed)
            both = restore(both)
            other, both = tie(other, both)
        if stage == 3:
            own, packed = tie(own, packed)
            mine = restore(own)
            other, mine = tie(other, mine)
        if stage == 4:
            predicted = pl.pallas_call(
                assemble,
                in_specs=[smem] + [vmem] * 4,
                out_shape=jax.ShapeDtypeStruct((total, sensors), F32),
                name="assemble",
                compiler_params=kernel_params(4),
            )(g, mine, core, chip, both)
            other, predicted = tie(other, predicted)
        packed = packed + other
    packed, chip_b = tie(packed, chip_b)
    both_b = lax.ppermute(chip_b, "grp", swapped("grp", 1))
    mixing_t = pl.pallas_call(
        functools.partial(solve_kernel, total - 1.0),
        out_shape=jax.ShapeDtypeStruct((members, total), F32),
        name="solve",
        compiler_params=kernel_params(4),
    )(packed)
    new = pl.pallas_call(
        update_kernel,
        in_specs=[smem] + [vmem] * 9,
        out_specs=anywhere,
        out_shape=jax.ShapeDtypeStruct((members * rows, columns), F32),
        scratch_shapes=[columns_of, pltpu.SemaphoreType.DMA((blocks,))],
        name="update",
        compiler_params=kernel_params(16),
    )(g, mixing_t, theta_a, core_a, chip_a, both_a, theta_b, core_b, chip_b, both_b)
    return (new.reshape(members, rows, columns), predicted)


def solution(mesh):
    return jax.shard_map(
        body,
        mesh=mesh,
        in_specs=(
            P("grp", "cell", None),
            P("grp", "cell", None),
            P("cell", None),
            P(None, "cell"),
            P("cell"),
        ),
        out_specs=(P("grp", "cell", None), P(None, "cell")),
        check_vma=False,
    )
```

```python
import functools

import jax
import jax.numpy as jnp
from jax import lax
from jax.experimental import pallas as pl
from jax.experimental.pallas import tpu as pltpu
from jax.sharding import PartitionSpec as P

LANES = 128
F32 = jnp.float32


def along(axis, shift):
    count = lax.axis_size(axis)
    return [(i, i + shift) for i in range(count) if 0 <= i + shift < count]


def swapped(axis, bit):
    return [(i, i ^ bit) for i in range(lax.axis_size(axis))]


def outflow(speed, rho):
    return 0.2 * (speed * rho * (1.0 - rho)) + 0.1 * rho


def from_left(x):
    lane = lax.broadcasted_iota(jnp.int32, x.shape, 1)
    return jnp.where(lane == 0, 0.0, pltpu.roll(x, 1, 1))


def from_right(x):
    last = x.shape[1] - 1
    lane = lax.broadcasted_iota(jnp.int32, x.shape, 1)
    return jnp.where(lane == last, 0.0, pltpu.roll(x, last, 1))


def without_above(rho, out, below):
    return 0.8 * rho - 2.0 * out + from_left(out) + 0.1 * (below + from_right(rho))


def box4(x):
    n = x.shape[1]
    pair = x + pltpu.roll(x, n - 1, 1)
    return pair + pltpu.roll(pair, n - 2, 1)


def load_columns(source, target, sems):
    copies = []
    for b in range(source.shape[1] // LANES):
        copy = pltpu.make_async_copy(source.at[:, pl.ds(b * LANES, LANES)], target.at[b], sems.at[b])
        copy.start()
        copies.append(copy)
    return copies


def prep_kernel(rows, odd, theta, rho, low_pair, high_pair, theta_a, theta_b, theta_in, rho_in, sems):
    waits = load_columns(rho, rho_in, sems.at[0]), load_columns(theta, theta_in, sems.at[1])
    members = low_pair.shape[0]
    half = theta_a.shape[0]
    swap = odd[0] == 1
    for b in range(theta_in.shape[0]):
        at = slice(b * LANES, (b + 1) * LANES)
        waits[0][b].wait()
        waits[1][b].wait()
        speed = [theta_in[b, pl.ds(r, members, stride=rows), :] for r in range(rows)]
        first, last = (rho_in[b, pl.ds(r, members, stride=rows), :] for r in (0, rows - 1))
        for r in range(rows):
            if r < half:
                theta_a[r, :, at] = speed[r]
            else:
                theta_b[r - half, :, at] = speed[r]
        down = outflow(speed[-1], last)
        low_pair[:, at] = jnp.where(swap, first, down)
        high_pair[:, at] = jnp.where(swap, down, first)


def rows_of(theta_a, theta_b, at):
    return [ref[r, at, :] for ref in (theta_a, theta_b) for r in range(ref.shape[0])]


def advance(speed, rho):
    out = [outflow(s, x) for s, x in zip(speed, rho)]
    new = []
    for r, x in enumerate(rho):
        under = rho[r + 1] + from_right(x) if r + 1 < len(rho) else from_right(x)
        y = 0.8 * x - 2.0 * out[r] + from_left(out[r]) + 0.1 * under
        new.append(y + out[r - 1] if r else y)
    return new, out


def inner1_kernel(theta_a, theta_b, rho, rho1, rho_in, sems):
    rows, members, _ = rho1.shape
    for b, copy in enumerate(load_columns(rho, rho_in, sems)):
        copy.wait()
        for r in range(rows):
            rho1[r, :, b * LANES : (b + 1) * LANES] = rho_in[b, pl.ds(r, members, stride=rows), :]

    def chunk(c, carry):
        at = pl.ds(c * 8, 8)
        new, _ = advance(rows_of(theta_a, theta_b, at), [rho1[r, at, :] for r in range(rows)])
        for r in range(rows):
            rho1[r, at, :] = new[r]
        return carry

    lax.fori_loop(0, members // 8, chunk, 0)


def edge1_kernel(odd, theta_a, theta_b, rho1, from_low, from_high, low_pair, high_pair, part, first, last):
    rows, members, _ = rho1.shape
    swap = odd[0] == 1

    def chunk(c, carry):
        at = pl.ds(c * 8, 8)
        low, high = from_low[at, :], from_high[at, :]
        top = rho1[0, at, :] + jnp.where(swap, low, high)
        bottom = rho1[rows - 1, at, :] + 0.1 * jnp.where(swap, high, low)
        down = outflow(theta_b[theta_b.shape[0] - 1, at, :], bottom)
        low_pair[at, :] = jnp.where(swap, top, down)
        high_pair[at, :] = jnp.where(swap, down, top)
        part[at, :] = without_above(top, outflow(theta_a[0, at, :], top), rho1[1, at, :])
        first[at, :] = top
        last[at, :] = bottom
        return carry

    lax.fori_loop(0, members // 8, chunk, 0)


def pick(table, first, last, low, high, pos_ref, start, out_ref):
    members = out_ref.shape[0]
    parts = members // 8
    width = 4
    for g0 in range(0, pos_ref.shape[0], width):
        groups = range(g0, g0 + width)
        where = [jnp.broadcast_to(pos_ref[g : g + 1, :], (8, LANES)) for g in groups]
        lane = [w & (LANES - 1) for w in where]
        block = [w >> 7 for w in where]
        begin = [jnp.maximum(low[g], first) for g in groups]
        trips = functools.reduce(
            jnp.maximum, [jnp.minimum(high[g], last) + 1 - lo for g, lo in zip(groups, begin)]
        )
        init = tuple(
            start[i * 8 : i * 8 + 8, g * LANES : (g + 1) * LANES] if start is not None else jnp.zeros((8, LANES), F32)
            for g in groups
            for i in range(parts)
        )

        def look(t, acc):
            new = []
            for k in range(width):
                p = begin[k] + t
                at = jnp.minimum(p, last) - first
                hit = block[k] == jnp.where(p <= last, p, -1)
                for i in range(parts):
                    row = table[at, i * 8 : i * 8 + 8, :]
                    got = jnp.take_along_axis(row, lane[k], axis=1, mode="promise_in_bounds")
                    new.append(jnp.where(hit, got, acc[k * parts + i]))
            return tuple(new)

        acc = lax.fori_loop(0, trips, look, init)
        for k, g in enumerate(groups):
            for i in range(parts):
                out_ref[i * 8 : i * 8 + 8, g * LANES : (g + 1) * LANES] = acc[k * parts + i]


def reorder_kernel(index, source, out, extra=None, extra_out=None):
    members = out.shape[0]
    groups = index.shape[0]

    def one(g, carry):
        where = jnp.broadcast_to(index[pl.ds(g, 1), :], (8, LANES))
        lane = where & (LANES - 1)
        block = where >> 7
        at = pl.ds(pl.multiple_of(g * LANES, LANES), LANES)
        for i in range(0, members, 8):
            acc = jnp.zeros((8, LANES), F32)
            for h in range(groups):
                row = source[i : i + 8, h * LANES : (h + 1) * LANES]
                got = jnp.take_along_axis(row, lane, axis=1, mode="promise_in_bounds")
                acc = jnp.where(block == h, got, acc)
            out[i : i + 8, at] = acc
        if extra is not None:
            acc = jnp.zeros((8, LANES), F32)
            for h in range(groups):
                row = jnp.broadcast_to(extra[:, h * LANES : (h + 1) * LANES], (8, LANES))
                got = jnp.take_along_axis(row, lane, axis=1, mode="promise_in_bounds")
                acc = jnp.where(block == h, got, acc)
            extra_out[:, at] = acc[:1]
        return carry

    lax.fori_loop(0, groups, one, 0)


def store_sums(table, row, at, x):
    sums = box4(x)
    blocks = x.shape[1] // LANES
    for b in range(blocks):
        table[row * blocks + b, at, :] = sums[:, b * LANES : (b + 1) * LANES]


def inner2_kernel(theta_a, theta_b, rho, first, last, pos, low, high, counts, head, tail, rest, table):
    rows, members, columns = rho.shape
    blocks = columns // LANES

    def chunk(c, carry):
        at = pl.ds(c * 8, 8)
        now = [first[at, :]] + [rho[r, at, :] for r in range(1, rows - 1)] + [last[at, :]]
        new, out = advance(rows_of(theta_a, theta_b, at), now)
        head[at, :] = new[0] + new[1]
        tail[at, :] = new[rows - 2] + new[rows - 1]
        rest[at, :] = new[rows - 1] + out[rows - 1]
        for r in range(1, rows - 2):
            store_sums(table, r - 1, at, new[r] + new[r + 1])
        return carry

    lax.fori_loop(0, members // 8, chunk, 0)
    pick(table, blocks, (rows - 2) * blocks - 1, low, high, pos, None, counts)


def edge2_kernel(rows, odd, head, tail, from_low, from_high, pos, low, high, counts, more, table):
    members, columns = head.shape
    blocks = columns // LANES
    swap = odd[0] == 1
    for c in range(0, members, 8):
        at = pl.ds(c, 8)
        one, two = from_low[at, :], from_high[at, :]
        store_sums(table, 0, at, head[at, :] + jnp.where(swap, one, two))
        store_sums(table, 1, at, tail[at, :] + 0.1 * jnp.where(swap, two, one))
    pick(table, 0, blocks - 1, low, high, pos, counts, more)
    pick(table.at[pl.ds(blocks, blocks)], (rows - 2) * blocks, (rows - 1) * blocks - 1, low, high, pos, more, more)


def finish_kernel(first, odd, rest, from_low, from_high, part, pos, low, high, counts, mine, table):
    members, columns = rest.shape
    blocks = columns // LANES
    swap = odd[0] == 1
    for c in range(0, members, 8):
        at = pl.ds(c, 8)
        beneath = jnp.where(swap, from_high[at, :], from_low[at, :])
        store_sums(table, 0, at, rest[at, :] + 0.1 * beneath + part[at, :])
    pick(table, first, first + blocks - 1, low, high, pos, counts, mine)


def pack(x, m, packed):
    n = 4 * m
    lane = lax.broadcasted_iota(jnp.int32, (m, n), 1)
    packed[0:m, :] = x[0:m]
    packed[m : 2 * m, :] = jnp.where(lane < m, pltpu.roll(x[3 * m : n], m, 1), x[m : 2 * m])
    half = m // 2
    low, high = x[2 * m : 2 * m + half], x[2 * m + half : 3 * m]
    packed[2 * m : 2 * m + half, :] = jnp.where(lane[:half] < 2 * m, pltpu.roll(high, 2 * m, 1), low)
    packed[2 * m + half :, :] = x[n:]


def unpack(packed, m):
    n = 4 * m
    half = m // 2
    second, third = packed[m : 2 * m, :], packed[2 * m : 2 * m + half, :]
    upper = jnp.concatenate(
        [packed[0:m, :], second, third, pltpu.roll(third, 2 * m, 1), pltpu.roll(second, 3 * m, 1)], axis=0
    )
    lane = lax.broadcasted_iota(jnp.int32, (n, n), 1)
    sub = lax.broadcasted_iota(jnp.int32, (n, n), 0)
    full = jnp.where(lane >= (sub & -m), upper, upper.T)
    return jnp.concatenate([full, packed[2 * m + half :, :]], axis=0)


def product_kernel(total, g_ref, own, core, chip, both, perturbed, noise, packed, every):
    members, sensors = own.shape
    g = g_ref[0]
    for step, piece in enumerate((own, core, chip, both)):
        every[pl.ds(pl.multiple_of((g ^ step) * members, members), members), :] = piece[...]
    width = 512
    acc = None
    for s in range(0, sensors, width):
        at = slice(s, s + width)
        counts = every[:, at]
        anomaly = counts - jnp.sum(counts, axis=0, keepdims=True) / total
        weighted = anomaly / noise[:, at]
        left = jnp.concatenate([anomaly, perturbed[:, at] - own[:, at]], axis=0)
        term = lax.dot_general(
            left, weighted, (((1,), (1,)), ((), ())), precision=lax.Precision.HIGHEST, preferred_element_type=F32
        )
        acc = term if acc is None else acc + term
    pack(acc, members, packed)


def lane_of(x, k):
    return jnp.take_along_axis(x, jnp.full(x.shape, k, jnp.int32), axis=1, mode="promise_in_bounds")


def sublane_of(x, r):
    return jnp.broadcast_to(x[r : r + 1, :], x.shape)


def solve_kernel(shift, packed, mixing_t):
    n = packed.shape[1]
    lane = lax.broadcasted_iota(jnp.int32, (8, n), 1)
    sub = lax.broadcasted_iota(jnp.int32, (8, n), 0)
    a = []
    wide = unpack(packed, n // 4)
    for i in range(wide.shape[0] // 8):
        x = wide[i * 8 : i * 8 + 8, :]
        a.append(jnp.where(lane == sub + i * 8, x + shift, x) if i * 8 < n else x)
    keep = jnp.zeros((8, n), F32)
    mix = jnp.zeros((8, n), F32)
    for k in range(0, n, 2):
        r = k % 8
        top = a[k // 8]
        c0, c1 = lane_of(top, k), lane_of(top, k + 1)
        r0, r1 = sublane_of(top, r), sublane_of(top, r + 1)
        p00, p01, p10, p11 = sublane_of(c0, r), sublane_of(c1, r), sublane_of(c0, r + 1), sublane_of(c1, r + 1)
        scale = 1.0 / (p00 * p11 - p01 * p10)
        here = (lane == k) | (lane == k + 1)
        f0 = jnp.where(here, 0.0, scale * (p11 * r0 - p01 * r1))
        f1 = jnp.where(here, 0.0, scale * (p00 * r1 - p10 * r0))
        keep = jnp.where(lane == k, scale * p11, jnp.where(lane == k + 1, scale * p00, keep))
        mix = jnp.where(lane == k, -(scale * p10), jnp.where(lane == k + 1, -(scale * p01), mix))
        for i in range(k // 8, len(a)):
            if i > k // 8:
                c0, c1 = lane_of(a[i], k), lane_of(a[i], k + 1)
            a[i] = a[i] - (c0 * f0 + c1 * f1)
    even = (lane & 1) == 0
    for i in range(n // 8, len(a)):
        x = a[i]
        other = jnp.where(even, pltpu.roll(x, n - 1, 1), pltpu.roll(x, 1, 1))
        w = x * keep + other * mix
        w = w - jnp.sum(w, axis=1, keepdims=True) / n
        at = i * 8 - n
        mixing_t[at : at + 8, :] = w


def split(x):
    high = x.astype(jnp.bfloat16)
    return high, (x - high.astype(F32)).astype(jnp.bfloat16)


def update_kernel(g_ref, mixing, *refs):
    pieces, (out, new, sems) = (refs[:4], refs[4:8]), refs[8:]
    half, members, columns = pieces[0][0].shape
    rows = half + pieces[1][0].shape[0]
    g = g_ref[0]
    wt = mixing[...]
    n = wt.shape[1]
    lane = lax.broadcasted_iota(jnp.int32, wt.shape, 1)
    crossed = jnp.where((lane & members) == 0, pltpu.roll(wt, n - members, 1), pltpu.roll(wt, members, 1))
    wt = jnp.where((g & 1) == 1, crossed, wt)
    wt = jnp.where((g & 2) == 2, pltpu.roll(wt, n // 2, 1), wt)
    wh, wl = split(wt)
    both = jnp.concatenate([wh, wl], axis=0)
    width = 2 * LANES
    sent = []
    for c in range(0, columns, width):
        for r in range(rows):
            x = [piece[r % half if r < half else r - half, :, c : c + width] for piece in pieces[r >= half]]
            xh, xl = split(jnp.concatenate(x, axis=0))
            high = jnp.dot(both, xh, preferred_element_type=F32)
            y = x[0] + (high[:members] + high[members:] + jnp.dot(wh, xl, preferred_element_type=F32))
            for k in range(width // LANES):
                new[c // LANES + k, pl.ds(r, members, stride=rows), :] = y[:, k * LANES : (k + 1) * LANES]
        for b in range(c // LANES, (c + width) // LANES):
            copy = pltpu.make_async_copy(new.at[b], out.at[:, pl.ds(b * LANES, LANES)], sems.at[b])
            copy.start()
            sent.append(copy)
    for copy in sent:
        copy.wait()


def tie(*values):
    return lax.optimization_barrier(values)


def kernel_params(mib):
    return pltpu.CompilerParams(vmem_limit_bytes=mib * 1024 * 1024)


def body(theta, density, footprint, perturbed, noise_var):
    members, rows, columns = theta.shape
    total = members * lax.axis_size("grp")
    sensors = footprint.shape[0]
    slab = rows * columns
    blocks = columns // LANES
    groups = sensors // LANES
    flat_theta = pltpu.with_memory_space_constraint(theta.reshape(members * rows, columns), pltpu.HBM)
    flat_rho = pltpu.with_memory_space_constraint(density.reshape(members * rows, columns), pltpu.HBM)
    g = lax.axis_index("grp").astype(jnp.int32).reshape(1)
    row = jax.ShapeDtypeStruct((members, columns), F32)
    turned = jax.ShapeDtypeStruct((rows, members, columns), F32)
    counts_shape = jax.ShapeDtypeStruct((members, sensors), F32)
    anywhere = pl.BlockSpec(memory_space=pltpu.HBM)
    vmem = pl.BlockSpec(memory_space=pltpu.VMEM)
    smem = pl.BlockSpec(memory_space=pltpu.SMEM)
    columns_of = pltpu.VMEM((blocks, members * rows, LANES), F32)

    odd = (lax.axis_index("cell") & 1).astype(jnp.int32).reshape(1)
    count = lax.axis_size("cell")
    far = [(i, i + 1 if i & 1 else i - 1) for i in range(1, count - 1)]

    def both_ways(low_pair, high_pair):
        from_low = lax.ppermute(low_pair, "cell", swapped("cell", 1))
        from_high = lax.ppermute(high_pair, "cell", far)
        return from_low, from_high

    early, late = (jax.ShapeDtypeStruct((n, members, columns), F32) for n in (rows * 3 // 8, rows - rows * 3 // 8))
    down, top, theta_a, theta_b = pl.pallas_call(
        functools.partial(prep_kernel, rows),
        in_specs=[smem, anywhere, anywhere],
        out_shape=[row, row, early, late],
        scratch_shapes=[columns_of, columns_of, pltpu.SemaphoreType.DMA((2, blocks))],
        name="prep",
        compiler_params=kernel_params(16),
    )(odd, flat_theta, flat_rho)
    above, below = both_ways(down, top)
    chip_a = lax.ppermute(theta_a, "grp", swapped("grp", 2))

    first = footprint[:, 0]
    rho1 = pl.pallas_call(
        inner1_kernel,
        in_specs=[vmem, vmem, anywhere],
        out_shape=turned,
        scratch_shapes=[columns_of, pltpu.SemaphoreType.DMA((blocks,))],
        name="inner1",
        compiler_params=kernel_params(12),
    )(theta_a, theta_b, flat_rho)
    rho1, first = tie(rho1, first)
    key = (first - lax.axis_index("cell") * slab) * sensors + lax.iota(jnp.int32, sensors)
    rank = jnp.sum((key[:, None] < key[None, :]).astype(jnp.int32), axis=0)
    chosen = rank[:, None] == lax.iota(jnp.int32, sensors)[None, :]
    ordered = jnp.sum(jnp.where(chosen, key[:, None], 0), axis=0)
    pos = (ordered // sensors).reshape(groups, LANES)
    order = (ordered & (sensors - 1)).reshape(groups, LANES)
    rank = rank.reshape(groups, LANES)
    low = pos[:, 0] >> 7
    high = pos[:, LANES - 1] >> 7
    above, below, pos, order, low, high, rank, rho1 = tie(above, below, pos, order, low, high, rank, rho1)

    low_pair, high_pair, part, first, last = pl.pallas_call(
        edge1_kernel,
        in_specs=[smem] + [vmem] * 5,
        out_shape=[row] * 5,
        name="edge1",
        compiler_params=kernel_params(12),
    )(odd, theta_a, theta_b, rho1, above, below)
    above, below = both_ways(low_pair, high_pair)
    part = lax.ppermute(part, "cell", along("cell", -1))

    counts, head, tail, rest = pl.pallas_call(
        inner2_kernel,
        in_specs=[vmem] * 6 + [smem] * 2,
        out_shape=[counts_shape, row, row, row],
        scratch_shapes=[pltpu.VMEM(((rows - 3) * blocks, members, LANES), F32)],
        name="inner2",
        compiler_params=kernel_params(14),
    )(theta_a, theta_b, rho1, first, last, pos, low, high)
    above, below, counts, head, tail, rest = tie(above, below, counts, head, tail, rest)
    counts = pl.pallas_call(
        functools.partial(edge2_kernel, rows),
        in_specs=[smem] + [vmem] * 5 + [smem] * 2 + [vmem],
        out_shape=counts_shape,
        scratch_shapes=[pltpu.VMEM((2 * blocks, members, LANES), F32)],
        name="edge2",
        compiler_params=kernel_params(6),
    )(odd, head, tail, above, below, pos, low, high, counts)
    counts, part = tie(counts, part)
    own = pl.pallas_call(
        functools.partial(finish_kernel, (rows - 1) * blocks),
        in_specs=[smem] + [vmem] * 5 + [smem] * 2 + [vmem],
        out_shape=counts_shape,
        scratch_shapes=[pltpu.VMEM((blocks, members, LANES), F32)],
        name="finish",
        compiler_params=kernel_params(6),
    )(odd, rest, above, below, part, pos, low, high, counts)

    def restore(counts):
        return pl.pallas_call(
            reorder_kernel, out_shape=counts_shape, name="restore", compiler_params=kernel_params(4)
        )(rank, counts)

    chip = lax.ppermute(own, "grp", swapped("grp", 2))
    core = lax.ppermute(own, "grp", swapped("grp", 1))
    own, perturbed, theta_a, theta_b = tie(own, perturbed, theta_a, theta_b)
    core_a = lax.ppermute(theta_a, "grp", swapped("grp", 1))
    core_b = lax.ppermute(theta_b, "grp", swapped("grp", 1))
    perturbed_own, noise = pl.pallas_call(
        lambda g, index, source, extra, out, extra_out: reorder_kernel(index, source, out, extra, extra_out),
        grid_spec=pltpu.PrefetchScalarGridSpec(
            num_scalar_prefetch=1,
            grid=(1,),
            in_specs=[
                pl.BlockSpec((groups, LANES), lambda i, g: (0, 0)),
                pl.BlockSpec((members, sensors), lambda i, g: (g[0], 0)),
                pl.BlockSpec((1, sensors), lambda i, g: (0, 0)),
            ],
            out_specs=[
                pl.BlockSpec((members, sensors), lambda i, g: (0, 0)),
                pl.BlockSpec((1, sensors), lambda i, g: (0, 0)),
            ],
        ),
        out_shape=[counts_shape, jax.ShapeDtypeStruct((1, sensors), F32)],
        name="reorder",
        compiler_params=kernel_params(4),
    )(g, order, perturbed, noise_var.reshape(1, sensors))
    chip, perturbed_own = tie(chip, perturbed_own)
    both = lax.ppermute(chip, "grp", swapped("grp", 1))
    core, chip_a, theta_b, chip = tie(core, chip_a, theta_b, chip)
    chip_b = lax.ppermute(theta_b, "grp", swapped("grp", 2))
    both_a = lax.ppermute(chip_a, "grp", swapped("grp", 1))
    packed = pl.pallas_call(
        functools.partial(product_kernel, total),
        in_specs=[smem] + [vmem] * 6,
        out_shape=jax.ShapeDtypeStruct((members * 7 // 2, total), F32),
        scratch_shapes=[pltpu.VMEM((total, sensors), F32)],
        name="product",
        compiler_params=kernel_params(12),
    )(g, own, core, chip, both, perturbed_own, noise)

    def assemble(g_ref, own, core, chip, both, out):
        g = g_ref[0]
        for step, piece in enumerate((own, core, chip, both)):
            out[pl.ds(pl.multiple_of((g ^ step) * members, members), members), :] = piece[...]

    for stage, bit in enumerate((1, 2, 8, 16, 4)):
        other = lax.ppermute(packed, "cell", swapped("cell", bit))
        if stage == 0:
            core, packed = tie(core, packed)
            core = restore(core)
            other, core = tie(other, core)
        if stage == 1:
            chip, packed = tie(chip, packed)
            chip = restore(chip)
            other, chip = tie(other, chip)
        if stage == 2:
            both, packed = tie(both, packed)
            both = restore(both)
            other, both = tie(other, both)
        if stage == 3:
            own, packed = tie(own, packed)
            mine = restore(own)
            other, mine = tie(other, mine)
        if stage == 4:
            predicted = pl.pallas_call(
                assemble,
                in_specs=[smem] + [vmem] * 4,
                out_shape=jax.ShapeDtypeStruct((total, sensors), F32),
                name="assemble",
                compiler_params=kernel_params(4),
            )(g, mine, core, chip, both)
            other, predicted = tie(other, predicted)
        packed = packed + other
    packed, chip_b = tie(packed, chip_b)
    both_b = lax.ppermute(chip_b, "grp", swapped("grp", 1))
    mixing_t = pl.pallas_call(
        functools.partial(solve_kernel, total - 1.0),
        out_shape=jax.ShapeDtypeStruct((members, total), F32),
        name="solve",
        compiler_params=kernel_params(4),
    )(packed)
    new = pl.pallas_call(
        update_kernel,
        in_specs=[smem] + [vmem] * 9,
        out_specs=anywhere,
        out_shape=jax.ShapeDtypeStruct((members * rows, columns), F32),
        scratch_shapes=[columns_of, pltpu.SemaphoreType.DMA((blocks,))],
        name="update",
        compiler_params=kernel_params(16),
    )(g, mixing_t, theta_a, core_a, chip_a, both_a, theta_b, core_b, chip_b, both_b)
    return (new.reshape(members, rows, columns), predicted)


def solution(mesh):
    return jax.shard_map(
        body,
        mesh=mesh,
        in_specs=(
            P("grp", "cell", None),
            P("grp", "cell", None),
            P("cell", None),
            P(None, "cell"),
            P("cell"),
        ),
        out_specs=(P("grp", "cell", None), P(None, "cell")),
        check_vma=False,
    )
```

```python
import functools

import jax
import jax.numpy as jnp
from jax import lax
from jax.experimental import pallas as pl
from jax.experimental.pallas import tpu as pltpu
from jax.sharding import PartitionSpec as P

LANES = 128
F32 = jnp.float32


def along(axis, shift):
    count = lax.axis_size(axis)
    return [(i, i + shift) for i in range(count) if 0 <= i + shift < count]


def swapped(axis, bit):
    return [(i, i ^ bit) for i in range(lax.axis_size(axis))]


def outflow(speed, rho):
    return 0.2 * (speed * rho * (1.0 - rho)) + 0.1 * rho


def from_left(x):
    lane = lax.broadcasted_iota(jnp.int32, x.shape, 1)
    return jnp.where(lane == 0, 0.0, pltpu.roll(x, 1, 1))


def from_right(x):
    last = x.shape[1] - 1
    lane = lax.broadcasted_iota(jnp.int32, x.shape, 1)
    return jnp.where(lane == last, 0.0, pltpu.roll(x, last, 1))


def without_above(rho, out, below):
    return 0.8 * rho - 2.0 * out + from_left(out) + 0.1 * (below + from_right(rho))


def box4(x):
    n = x.shape[1]
    pair = x + pltpu.roll(x, n - 1, 1)
    return pair + pltpu.roll(pair, n - 2, 1)


def load_columns(source, target, sems):
    copies = []
    for b in range(source.shape[1] // LANES):
        copy = pltpu.make_async_copy(source.at[:, pl.ds(b * LANES, LANES)], target.at[b], sems.at[b])
        copy.start()
        copies.append(copy)
    return copies


def prep_kernel(rows, odd, theta, rho, low_pair, high_pair, theta_a, theta_b, theta_in, rho_in, sems):
    waits = load_columns(rho, rho_in, sems.at[0]), load_columns(theta, theta_in, sems.at[1])
    members = low_pair.shape[0]
    half = theta_a.shape[0]
    swap = odd[0] == 1
    for b in range(theta_in.shape[0]):
        at = slice(b * LANES, (b + 1) * LANES)
        waits[0][b].wait()
        waits[1][b].wait()
        speed = [theta_in[b, pl.ds(r, members, stride=rows), :] for r in range(rows)]
        first, last = (rho_in[b, pl.ds(r, members, stride=rows), :] for r in (0, rows - 1))
        for r in range(rows):
            if r < half:
                theta_a[r, :, at] = speed[r]
            else:
                theta_b[r - half, :, at] = speed[r]
        down = outflow(speed[-1], last)
        low_pair[:, at] = jnp.where(swap, first, down)
        high_pair[:, at] = jnp.where(swap, down, first)


def rows_of(theta_a, theta_b, at):
    return [ref[r, at, :] for ref in (theta_a, theta_b) for r in range(ref.shape[0])]


def advance(speed, rho):
    out = [outflow(s, x) for s, x in zip(speed, rho)]
    new = []
    for r, x in enumerate(rho):
        under = rho[r + 1] + from_right(x) if r + 1 < len(rho) else from_right(x)
        y = 0.8 * x - 2.0 * out[r] + from_left(out[r]) + 0.1 * under
        new.append(y + out[r - 1] if r else y)
    return new, out


def inner1_kernel(theta_a, theta_b, rho, rho1, rho_in, sems):
    rows, members, _ = rho1.shape
    for b, copy in enumerate(load_columns(rho, rho_in, sems)):
        copy.wait()
        for r in range(rows):
            rho1[r, :, b * LANES : (b + 1) * LANES] = rho_in[b, pl.ds(r, members, stride=rows), :]

    def chunk(c, carry):
        at = pl.ds(c * 8, 8)
        new, _ = advance(rows_of(theta_a, theta_b, at), [rho1[r, at, :] for r in range(rows)])
        for r in range(rows):
            rho1[r, at, :] = new[r]
        return carry

    lax.fori_loop(0, members // 8, chunk, 0)


def edge1_kernel(odd, theta_a, theta_b, rho1, from_low, from_high, low_pair, high_pair, part, first, last):
    rows, members, _ = rho1.shape
    swap = odd[0] == 1

    def chunk(c, carry):
        at = pl.ds(c * 8, 8)
        low, high = from_low[at, :], from_high[at, :]
        top = rho1[0, at, :] + jnp.where(swap, low, high)
        bottom = rho1[rows - 1, at, :] + 0.1 * jnp.where(swap, high, low)
        down = outflow(theta_b[theta_b.shape[0] - 1, at, :], bottom)
        low_pair[at, :] = jnp.where(swap, top, down)
        high_pair[at, :] = jnp.where(swap, down, top)
        part[at, :] = without_above(top, outflow(theta_a[0, at, :], top), rho1[1, at, :])
        first[at, :] = top
        last[at, :] = bottom
        return carry

    lax.fori_loop(0, members // 8, chunk, 0)


def pick(table, first, last, low, high, pos_ref, start, out_ref):
    members = out_ref.shape[0]
    parts = members // 8
    width = 4
    for g0 in range(0, pos_ref.shape[0], width):
        groups = range(g0, g0 + width)
        where = [jnp.broadcast_to(pos_ref[g : g + 1, :], (8, LANES)) for g in groups]
        lane = [w & (LANES - 1) for w in where]
        block = [w >> 7 for w in where]
        begin = [jnp.maximum(low[g], first) for g in groups]
        trips = functools.reduce(
            jnp.maximum, [jnp.minimum(high[g], last) + 1 - lo for g, lo in zip(groups, begin)]
        )
        init = tuple(
            start[i * 8 : i * 8 + 8, g * LANES : (g + 1) * LANES] if start is not None else jnp.zeros((8, LANES), F32)
            for g in groups
            for i in range(parts)
        )

        def look(t, acc):
            new = []
            for k in range(width):
                p = begin[k] + t
                at = jnp.minimum(p, last) - first
                hit = block[k] == jnp.where(p <= last, p, -1)
                for i in range(parts):
                    row = table[at, i * 8 : i * 8 + 8, :]
                    got = jnp.take_along_axis(row, lane[k], axis=1, mode="promise_in_bounds")
                    new.append(jnp.where(hit, got, acc[k * parts + i]))
            return tuple(new)

        acc = lax.fori_loop(0, trips, look, init)
        for k, g in enumerate(groups):
            for i in range(parts):
                out_ref[i * 8 : i * 8 + 8, g * LANES : (g + 1) * LANES] = acc[k * parts + i]


def reorder_kernel(index, source, out, extra=None, extra_out=None):
    members = out.shape[0]
    groups = index.shape[0]

    def one(g, carry):
        where = jnp.broadcast_to(index[pl.ds(g, 1), :], (8, LANES))
        lane = where & (LANES - 1)
        block = where >> 7
        at = pl.ds(pl.multiple_of(g * LANES, LANES), LANES)
        for i in range(0, members, 8):
            acc = jnp.zeros((8, LANES), F32)
            for h in range(groups):
                row = source[i : i + 8, h * LANES : (h + 1) * LANES]
                got = jnp.take_along_axis(row, lane, axis=1, mode="promise_in_bounds")
                acc = jnp.where(block == h, got, acc)
            out[i : i + 8, at] = acc
        if extra is not None:
            acc = jnp.zeros((8, LANES), F32)
            for h in range(groups):
                row = jnp.broadcast_to(extra[:, h * LANES : (h + 1) * LANES], (8, LANES))
                got = jnp.take_along_axis(row, lane, axis=1, mode="promise_in_bounds")
                acc = jnp.where(block == h, got, acc)
            extra_out[:, at] = acc[:1]
        return carry

    lax.fori_loop(0, groups, one, 0)


def store_sums(table, row, at, x):
    sums = box4(x)
    blocks = x.shape[1] // LANES
    for b in range(blocks):
        table[row * blocks + b, at, :] = sums[:, b * LANES : (b + 1) * LANES]


def inner2_kernel(theta_a, theta_b, rho, first, last, pos, low, high, counts, head, tail, rest, table):
    rows, members, columns = rho.shape
    blocks = columns // LANES

    def chunk(c, carry):
        at = pl.ds(c * 8, 8)
        now = [first[at, :]] + [rho[r, at, :] for r in range(1, rows - 1)] + [last[at, :]]
        new, out = advance(rows_of(theta_a, theta_b, at), now)
        head[at, :] = new[0] + new[1]
        tail[at, :] = new[rows - 2] + new[rows - 1]
        rest[at, :] = new[rows - 1] + out[rows - 1]
        for r in range(1, rows - 2):
            store_sums(table, r - 1, at, new[r] + new[r + 1])
        return carry

    lax.fori_loop(0, members // 8, chunk, 0)
    pick(table, blocks, (rows - 2) * blocks - 1, low, high, pos, None, counts)


def edge2_kernel(rows, odd, head, tail, from_low, from_high, pos, low, high, counts, more, table):
    members, columns = head.shape
    blocks = columns // LANES
    swap = odd[0] == 1
    for c in range(0, members, 8):
        at = pl.ds(c, 8)
        one, two = from_low[at, :], from_high[at, :]
        store_sums(table, 0, at, head[at, :] + jnp.where(swap, one, two))
        store_sums(table, 1, at, tail[at, :] + 0.1 * jnp.where(swap, two, one))
    pick(table, 0, blocks - 1, low, high, pos, counts, more)
    pick(table.at[pl.ds(blocks, blocks)], (rows - 2) * blocks, (rows - 1) * blocks - 1, low, high, pos, more, more)


def finish_kernel(first, odd, rest, from_low, from_high, part, pos, low, high, counts, mine, table):
    members, columns = rest.shape
    blocks = columns // LANES
    swap = odd[0] == 1
    for c in range(0, members, 8):
        at = pl.ds(c, 8)
        beneath = jnp.where(swap, from_high[at, :], from_low[at, :])
        store_sums(table, 0, at, rest[at, :] + 0.1 * beneath + part[at, :])
    pick(table, first, first + blocks - 1, low, high, pos, counts, mine)


def pack(x, m, packed):
    n = 4 * m
    lane = lax.broadcasted_iota(jnp.int32, (m, n), 1)
    packed[0:m, :] = x[0:m]
    packed[m : 2 * m, :] = jnp.where(lane < m, pltpu.roll(x[3 * m : n], m, 1), x[m : 2 * m])
    half = m // 2
    low, high = x[2 * m : 2 * m + half], x[2 * m + half : 3 * m]
    packed[2 * m : 2 * m + half, :] = jnp.where(lane[:half] < 2 * m, pltpu.roll(high, 2 * m, 1), low)
    packed[2 * m + half :, :] = x[n:]


def unpack(packed, m):
    n = 4 * m
    half = m // 2
    second, third = packed[m : 2 * m, :], packed[2 * m : 2 * m + half, :]
    upper = jnp.concatenate(
        [packed[0:m, :], second, third, pltpu.roll(third, 2 * m, 1), pltpu.roll(second, 3 * m, 1)], axis=0
    )
    lane = lax.broadcasted_iota(jnp.int32, (n, n), 1)
    sub = lax.broadcasted_iota(jnp.int32, (n, n), 0)
    full = jnp.where(lane >= (sub & -m), upper, upper.T)
    return jnp.concatenate([full, packed[2 * m + half :, :]], axis=0)


def product_kernel(total, g_ref, own, core, chip, both, perturbed, noise, packed, every):
    members, sensors = own.shape
    g = g_ref[0]
    for step, piece in enumerate((own, core, chip, both)):
        every[pl.ds(pl.multiple_of((g ^ step) * members, members), members), :] = piece[...]
    width = 512
    acc = None
    for s in range(0, sensors, width):
        at = slice(s, s + width)
        counts = every[:, at]
        anomaly = counts - jnp.sum(counts, axis=0, keepdims=True) / total
        weighted = anomaly / noise[:, at]
        left = jnp.concatenate([anomaly, perturbed[:, at] - own[:, at]], axis=0)
        term = lax.dot_general(
            left, weighted, (((1,), (1,)), ((), ())), precision=lax.Precision.HIGHEST, preferred_element_type=F32
        )
        acc = term if acc is None else acc + term
    pack(acc, members, packed)


def lane_of(x, k):
    return jnp.take_along_axis(x, jnp.full(x.shape, k, jnp.int32), axis=1, mode="promise_in_bounds")


def sublane_of(x, r):
    return jnp.broadcast_to(x[r : r + 1, :], x.shape)


def solve_kernel(shift, packed, mixing_t):
    n = packed.shape[1]
    lane = lax.broadcasted_iota(jnp.int32, (8, n), 1)
    sub = lax.broadcasted_iota(jnp.int32, (8, n), 0)
    a = []
    wide = unpack(packed, n // 4)
    for i in range(wide.shape[0] // 8):
        x = wide[i * 8 : i * 8 + 8, :]
        a.append(jnp.where(lane == sub + i * 8, x + shift, x) if i * 8 < n else x)
    keep = jnp.zeros((8, n), F32)
    mix = jnp.zeros((8, n), F32)
    for k in range(0, n, 2):
        r = k % 8
        top = a[k // 8]
        c0, c1 = lane_of(top, k), lane_of(top, k + 1)
        r0, r1 = sublane_of(top, r), sublane_of(top, r + 1)
        p00, p01, p10, p11 = sublane_of(c0, r), sublane_of(c1, r), sublane_of(c0, r + 1), sublane_of(c1, r + 1)
        scale = 1.0 / (p00 * p11 - p01 * p10)
        here = (lane == k) | (lane == k + 1)
        f0 = jnp.where(here, 0.0, scale * (p11 * r0 - p01 * r1))
        f1 = jnp.where(here, 0.0, scale * (p00 * r1 - p10 * r0))
        keep = jnp.where(lane == k, scale * p11, jnp.where(lane == k + 1, scale * p00, keep))
        mix = jnp.where(lane == k, -(scale * p10), jnp.where(lane == k + 1, -(scale * p01), mix))
        for i in range(k // 8, len(a)):
            if i > k // 8:
                c0, c1 = lane_of(a[i], k), lane_of(a[i], k + 1)
            a[i] = a[i] - (c0 * f0 + c1 * f1)
    even = (lane & 1) == 0
    for i in range(n // 8, len(a)):
        x = a[i]
        other = jnp.where(even, pltpu.roll(x, n - 1, 1), pltpu.roll(x, 1, 1))
        w = x * keep + other * mix
        w = w - jnp.sum(w, axis=1, keepdims=True) / n
        at = i * 8 - n
        mixing_t[at : at + 8, :] = w


def split(x):
    high = x.astype(jnp.bfloat16)
    return high, (x - high.astype(F32)).astype(jnp.bfloat16)


def update_kernel(g_ref, mixing, *refs):
    pieces, (out, new, sems) = (refs[:4], refs[4:8]), refs[8:]
    half, members, columns = pieces[0][0].shape
    rows = half + pieces[1][0].shape[0]
    g = g_ref[0]
    wt = mixing[...]
    n = wt.shape[1]
    lane = lax.broadcasted_iota(jnp.int32, wt.shape, 1)
    crossed = jnp.where((lane & members) == 0, pltpu.roll(wt, n - members, 1), pltpu.roll(wt, members, 1))
    wt = jnp.where((g & 1) == 1, crossed, wt)
    wt = jnp.where((g & 2) == 2, pltpu.roll(wt, n // 2, 1), wt)
    wh, wl = split(wt)
    both = jnp.concatenate([wh, wl], axis=0)
    width = 2 * LANES
    sent = []
    for c in range(0, columns, width):
        for r in range(rows):
            x = [piece[r % half if r < half else r - half, :, c : c + width] for piece in pieces[r >= half]]
            xh, xl = split(jnp.concatenate(x, axis=0))
            high = jnp.dot(both, xh, preferred_element_type=F32)
            y = x[0] + (high[:members] + high[members:] + jnp.dot(wh, xl, preferred_element_type=F32))
            for k in range(width // LANES):
                new[c // LANES + k, pl.ds(r, members, stride=rows), :] = y[:, k * LANES : (k + 1) * LANES]
        for b in range(c // LANES, (c + width) // LANES):
            copy = pltpu.make_async_copy(new.at[b], out.at[:, pl.ds(b * LANES, LANES)], sems.at[b])
            copy.start()
            sent.append(copy)
    for copy in sent:
        copy.wait()


def hold_kernel(source, out):
    out[...] = source[...]


def tie(*values):
    return lax.optimization_barrier(values)


def kernel_params(mib):
    return pltpu.CompilerParams(vmem_limit_bytes=mib * 1024 * 1024)


def body(theta, density, footprint, perturbed, noise_var):
    members, rows, columns = theta.shape
    total = members * lax.axis_size("grp")
    sensors = footprint.shape[0]
    slab = rows * columns
    blocks = columns // LANES
    groups = sensors // LANES
    flat_theta = pltpu.with_memory_space_constraint(theta.reshape(members * rows, columns), pltpu.HBM)
    flat_rho = pltpu.with_memory_space_constraint(density.reshape(members * rows, columns), pltpu.HBM)
    g = lax.axis_index("grp").astype(jnp.int32).reshape(1)
    row = jax.ShapeDtypeStruct((members, columns), F32)
    turned = jax.ShapeDtypeStruct((rows, members, columns), F32)
    counts_shape = jax.ShapeDtypeStruct((members, sensors), F32)
    anywhere = pl.BlockSpec(memory_space=pltpu.HBM)
    vmem = pl.BlockSpec(memory_space=pltpu.VMEM)
    smem = pl.BlockSpec(memory_space=pltpu.SMEM)
    columns_of = pltpu.VMEM((blocks, members * rows, LANES), F32)

    odd = (lax.axis_index("cell") & 1).astype(jnp.int32).reshape(1)
    count = lax.axis_size("cell")
    far = [(i, i + 1 if i & 1 else i - 1) for i in range(1, count - 1)]

    def both_ways(low_pair, high_pair):
        from_low = lax.ppermute(low_pair, "cell", swapped("cell", 1))
        from_high = lax.ppermute(high_pair, "cell", far)
        return from_low, from_high

    early, late = (jax.ShapeDtypeStruct((n, members, columns), F32) for n in (rows * 3 // 8, rows - rows * 3 // 8))
    down, top, theta_a, theta_b = pl.pallas_call(
        functools.partial(prep_kernel, rows),
        in_specs=[smem, anywhere, anywhere],
        out_shape=[row, row, early, late],
        scratch_shapes=[columns_of, columns_of, pltpu.SemaphoreType.DMA((2, blocks))],
        name="prep",
        compiler_params=kernel_params(16),
    )(odd, flat_theta, flat_rho)
    above, below = both_ways(down, top)
    chip_a = lax.ppermute(theta_a, "grp", swapped("grp", 2))

    first = footprint[:, 0]
    rho1 = pl.pallas_call(
        inner1_kernel,
        in_specs=[vmem, vmem, anywhere],
        out_shape=turned,
        scratch_shapes=[columns_of, pltpu.SemaphoreType.DMA((blocks,))],
        name="inner1",
        compiler_params=kernel_params(12),
    )(theta_a, theta_b, flat_rho)
    rho1, first = tie(rho1, first)
    key = (first - lax.axis_index("cell") * slab) * sensors + lax.iota(jnp.int32, sensors)
    rank = jnp.sum((key[:, None] < key[None, :]).astype(jnp.int32), axis=0)
    chosen = rank[:, None] == lax.iota(jnp.int32, sensors)[None, :]
    ordered = jnp.sum(jnp.where(chosen, key[:, None], 0), axis=0)
    pos = (ordered // sensors).reshape(groups, LANES)
    order = (ordered & (sensors - 1)).reshape(groups, LANES)
    rank = rank.reshape(groups, LANES)
    low = pos[:, 0] >> 7
    high = pos[:, LANES - 1] >> 7
    above, below, pos, order, low, high, rank, rho1 = tie(above, below, pos, order, low, high, rank, rho1)

    low_pair, high_pair, part, first, last = pl.pallas_call(
        edge1_kernel,
        in_specs=[smem] + [vmem] * 5,
        out_shape=[row] * 5,
        name="edge1",
        compiler_params=kernel_params(12),
    )(odd, theta_a, theta_b, rho1, above, below)
    above, below = both_ways(low_pair, high_pair)
    part = lax.ppermute(part, "cell", along("cell", -1))

    counts, head, tail, rest = pl.pallas_call(
        inner2_kernel,
        in_specs=[vmem] * 6 + [smem] * 2,
        out_shape=[counts_shape, row, row, row],
        scratch_shapes=[pltpu.VMEM(((rows - 3) * blocks, members, LANES), F32)],
        name="inner2",
        compiler_params=kernel_params(14),
    )(theta_a, theta_b, rho1, first, last, pos, low, high)
    above, below, counts, head, tail, rest = tie(above, below, counts, head, tail, rest)
    counts = pl.pallas_call(
        functools.partial(edge2_kernel, rows),
        in_specs=[smem] + [vmem] * 5 + [smem] * 2 + [vmem],
        out_shape=counts_shape,
        scratch_shapes=[pltpu.VMEM((2 * blocks, members, LANES), F32)],
        name="edge2",
        compiler_params=kernel_params(6),
    )(odd, head, tail, above, below, pos, low, high, counts)
    counts, part = tie(counts, part)
    own = pl.pallas_call(
        functools.partial(finish_kernel, (rows - 1) * blocks),
        in_specs=[smem] + [vmem] * 5 + [smem] * 2 + [vmem],
        out_shape=counts_shape,
        scratch_shapes=[pltpu.VMEM((blocks, members, LANES), F32)],
        name="finish",
        compiler_params=kernel_params(6),
    )(odd, rest, above, below, part, pos, low, high, counts)

    def restore(counts):
        return pl.pallas_call(
            reorder_kernel, out_shape=counts_shape, name="restore", compiler_params=kernel_params(4)
        )(rank, counts)

    chip = lax.ppermute(own, "grp", swapped("grp", 2))
    core = lax.ppermute(own, "grp", swapped("grp", 1))
    own, perturbed, theta_a, theta_b = tie(own, perturbed, theta_a, theta_b)
    core_a = lax.ppermute(theta_a, "grp", swapped("grp", 1))
    core_b = lax.ppermute(theta_b, "grp", swapped("grp", 1))
    perturbed_own, noise = pl.pallas_call(
        lambda g, index, source, extra, out, extra_out: reorder_kernel(index, source, out, extra, extra_out),
        grid_spec=pltpu.PrefetchScalarGridSpec(
            num_scalar_prefetch=1,
            grid=(1,),
            in_specs=[
                pl.BlockSpec((groups, LANES), lambda i, g: (0, 0)),
                pl.BlockSpec((members, sensors), lambda i, g: (g[0], 0)),
                pl.BlockSpec((1, sensors), lambda i, g: (0, 0)),
            ],
            out_specs=[
                pl.BlockSpec((members, sensors), lambda i, g: (0, 0)),
                pl.BlockSpec((1, sensors), lambda i, g: (0, 0)),
            ],
        ),
        out_shape=[counts_shape, jax.ShapeDtypeStruct((1, sensors), F32)],
        name="reorder",
        compiler_params=kernel_params(4),
    )(g, order, perturbed, noise_var.reshape(1, sensors))
    chip, perturbed_own = tie(chip, perturbed_own)
    both = lax.ppermute(chip, "grp", swapped("grp", 1))
    core, chip_a, theta_b, chip = tie(core, chip_a, theta_b, chip)
    chip_b = lax.ppermute(theta_b, "grp", swapped("grp", 2))
    both_a = lax.ppermute(chip_a, "grp", swapped("grp", 1))
    packed = pl.pallas_call(
        functools.partial(product_kernel, total),
        in_specs=[smem] + [vmem] * 6,
        out_shape=jax.ShapeDtypeStruct((members * 7 // 2, total), F32),
        scratch_shapes=[pltpu.VMEM((total, sensors), F32)],
        name="product",
        compiler_params=kernel_params(12),
    )(g, own, core, chip, both, perturbed_own, noise)

    def assemble(g_ref, own, core, chip, both, out):
        g = g_ref[0]
        for step, piece in enumerate((own, core, chip, both)):
            out[pl.ds(pl.multiple_of((g ^ step) * members, members), members), :] = piece[...]

    for stage, bit in enumerate((1, 2, 8, 16, 4)):
        other = lax.ppermute(packed, "cell", swapped("cell", bit))
        if stage == 0:
            core, packed = tie(core, packed)
            core = restore(core)
            other, core = tie(other, core)
        if stage == 1:
            chip, packed = tie(chip, packed)
            chip = restore(chip)
            other, chip = tie(other, chip)
        if stage == 2:
            both, packed = tie(both, packed)
            both = restore(both)
            other, both = tie(other, both)
        if stage == 3:
            own, packed = tie(own, packed)
            mine = restore(own)
            other, mine = tie(other, mine)
        if stage == 4:
            chip_a, both_a, packed = tie(chip_a, both_a, packed)
            chip_a = pl.pallas_call(
                hold_kernel,
                in_specs=[vmem],
                out_shape=jax.ShapeDtypeStruct(chip_a.shape, F32),
                name="hold",
                compiler_params=kernel_params(4),
            )(chip_a)
            other, chip_a = tie(other, chip_a)
            predicted = pl.pallas_call(
                assemble,
                in_specs=[smem] + [vmem] * 4,
                out_shape=jax.ShapeDtypeStruct((total, sensors), F32),
                name="assemble",
                compiler_params=kernel_params(4),
            )(g, mine, core, chip, both)
            other, predicted = tie(other, predicted)
        packed = packed + other
    packed, chip_b = tie(packed, chip_b)
    both_b = lax.ppermute(chip_b, "grp", swapped("grp", 1))
    mixing_t = pl.pallas_call(
        functools.partial(solve_kernel, total - 1.0),
        out_shape=jax.ShapeDtypeStruct((members, total), F32),
        name="solve",
        compiler_params=kernel_params(4),
    )(packed)
    new = pl.pallas_call(
        update_kernel,
        in_specs=[smem] + [vmem] * 9,
        out_specs=anywhere,
        out_shape=jax.ShapeDtypeStruct((members * rows, columns), F32),
        scratch_shapes=[columns_of, pltpu.SemaphoreType.DMA((blocks,))],
        name="update",
        compiler_params=kernel_params(16),
    )(g, mixing_t, theta_a, core_a, chip_a, both_a, theta_b, core_b, chip_b, both_b)
    return (new.reshape(members, rows, columns), predicted)


def solution(mesh):
    return jax.shard_map(
        body,
        mesh=mesh,
        in_specs=(
            P("grp", "cell", None),
            P("grp", "cell", None),
            P("cell", None),
            P(None, "cell"),
            P("cell"),
        ),
        out_specs=(P("grp", "cell", None), P(None, "cell")),
        check_vma=False,
    )
```
